256 devices in a mesh: dp: 32 (over z, x), seq: 8 (over y, core).
Axes of the slice: x: 4, y: 4, z: 8, core: 2. Of those that a mesh axis runs over, the one named last changes fastest.
Arguments:
- residual_tiles: bfloat16 [32, 2048, 1024], P('dp', 'seq'), may hold values from -16 to 16
- picture_label_tile: int32 [32, 2048], P('dp', 'seq'), may hold values from 0 to 11, never falling along the last dimension, each value on 1 to 1024 neighbouring positions
- prenorm_multiplier: float32 [1024], replicated, may hold values from 0.5 to 1.5
- triple_projector: bfloat16 [1024, 3072], P('dp'), may hold values from -0.25 to 0.25
- logit_scaling: float32 [16], replicated, may hold values from 0.3 to 30
- final_projector: bfloat16 [1024, 1024], P('dp'), may hold values from -0.1875 to 0.1875
- binarizer_projector: bfloat16 [1024, 18], replicated, may hold values from -0.1875 to 0.1875
- binarizer_offset: float32 [18], replicated, may hold values from -1 to 1
Outputs:
- mixed: bfloat16 [32, 2048, 1024], P('dp', 'seq')
- bit_codes: float32 [32, 18, 2048], P('dp', None, 'seq')
- code_entropy: float32 [18], replicated
The draws below stay inside these ranges and needn't reach their ends.
Inputs may be any that keep to these rules, and one draw needn't show every extreme that they name: `picture_label_tile`: in each pack image numbers never fall, every image number of 0 to 11 occurs, and an image has at most 1024 patches.
All inputs are finite; a program needn't handle non-finite values.
Results may differ from the reference program's by a relative error of at most 0.0053.
The reference program's roundings to bfloat16 on the way count: a program that leaves them out, or rounds other values in their place, can miss the bound.
Values may be sent and summed in bfloat16 or wider, within the bound.
No kernel may reach another device: no remote copies, remote signals or barrier semaphores. Data moves between devices by JAX's collectives and lax.ppermute only.
A program may use at most 64 MiB of HBM per device.

```python
import math
import jax
import jax.numpy as jnp
import numpy as np
from jax import lax

D = 1024
HEADS = 16
CHANNEL_COUNT = 64
BITS = 18
IMAGES = 12
SEQ = 2048
PACKS = 32


def draw_residual_tiles(key, part):
    first_key, second_key = jax.random.split(key, 2)
    pack_place = jnp.arange(PACKS, dtype=jnp.float32) / max(PACKS - 1, 1)
    token_place = jnp.arange(SEQ, dtype=jnp.float32) / max(SEQ - 1, 1)
    trend = jnp.exp(jnp.log(3.0) * pack_place)[:, None] * jnp.exp(jnp.log(2.0) * token_place)[None, :]
    rough = jnp.exp(jax.random.uniform(first_key, (PACKS, SEQ), minval=jnp.log(0.4), maxval=jnp.log(1.6)))
    base = jax.random.normal(second_key, (PACKS, SEQ, D))
    values = base * (trend * rough)[:, :, None] * 0.5
    return jnp.clip(values, -16.0, 16.0).astype(jnp.bfloat16)


def draw_triple_projector(key, part):
    first_key = jax.random.fold_in(key, 0)
    spread = D ** (-0.5)
    base = jax.random.normal(first_key, (D, 3, D)) * spread
    return jnp.clip(base.reshape(D, 3 * D), -0.25, 0.25).astype(jnp.bfloat16)


def draw_logit_scaling(key, part):
    first_key = jax.random.fold_in(key, 0)
    values = jnp.exp(jax.random.uniform(first_key, (HEADS,), minval=jnp.log(0.3), maxval=jnp.log(3.0)))
    return values.astype(jnp.float32)


def steps_of(key, extent, shards, smallest, largest):
    level, own = 1.0, jax.random.fold_in(key, 6)
    for dim, shards_of in shards:
        draws = jnp.exp(jax.random.uniform(jax.random.fold_in(own, dim), (shards_of,), jnp.float32, smallest / len(shards), largest / len(shards)))
        level = level * jnp.repeat(draws, extent[dim] // shards_of).reshape([-1 if axis == dim else 1 for axis in range(len(extent))])
    return level


def profile(amount, total, reach, lean):
    portions = [(1 << 20) // math.isqrt(rank ** lean) + 1 for rank in range(2, amount + 1)]
    surplus, holding = total - reach - (amount - 1), [1] * (amount - 1)
    while surplus > 0:
        free = [i for i in range(amount - 1) if holding[i] < reach]
        whole, budget = sum([portions[i] for i in free]), surplus
        for i in free:
            more = min(reach - holding[i], max(1, budget * portions[i] // whole), surplus)
            holding[i] = holding[i] + more
            surplus = surplus - more
    return np.array([reach] + holding)


def uneven(rng, number_of, total, limit, slope):
    if number_of == 2:
        one = jax.random.randint(rng, (), max(1, total - limit), min(limit, total - 1) + 1)
        return jnp.stack([one, total - one])
    sizes = jnp.asarray(profile(number_of, total, limit, slope), jnp.int32)
    twos = (number_of - 1) // 2
    donor, taker = sizes[1:1 + 2 * twos:2], sizes[2:2 + 2 * twos:2]
    margin = jnp.minimum(donor - 1, limit - taker)
    shifted = jax.random.randint(jax.random.fold_in(rng, 1), (twos,), 0, 1 << 20) % (margin + 1)
    sizes = sizes.at[1:1 + 2 * twos:2].set(donor - shifted).at[2:2 + 2 * twos:2].set(taker + shifted)
    return sizes[jax.random.permutation(jax.random.fold_in(rng, 2), number_of)]


def gaussian(stream_key, extent, scale, reach, cuts=(), kind=jnp.bfloat16):
    factor_of = steps_of(stream_key, extent, cuts, -0.22, 0.18) if cuts else 1.0
    result = jax.random.normal(stream_key, extent, jnp.float32) * scale * factor_of
    return jnp.minimum(jnp.maximum(result, -reach), reach).astype(kind)


def setup_inputs(seed: int = 0) -> dict:
    keys = jax.random.split(jax.random.key(seed), 9)
    return {
        "residual_tiles": draw_residual_tiles(jax.random.fold_in(keys[8], 71), 0),
        "picture_label_tile": jax.vmap(lambda own: jnp.searchsorted(jnp.cumsum(uneven(own, IMAGES, SEQ, SEQ // 2, 2)), jnp.arange(SEQ), side="right"))(jax.random.split(keys[1], PACKS)).reshape((PACKS, SEQ)).astype(jnp.int32),
        "prenorm_multiplier": jnp.clip(1.0 + 0.1 * jax.random.normal(keys[2], (D,), jnp.float32), 0.5, 1.5),
        "triple_projector": draw_triple_projector(jax.random.fold_in(keys[8], 71), 0),
        "logit_scaling": draw_logit_scaling(jax.random.fold_in(keys[8], 71), 0),
        "final_projector": gaussian(keys[5], (D, D), D ** -0.5, 0.1875, ((0, 32),)),
        "binarizer_projector": gaussian(keys[6], (D, BITS), D ** -0.5, 0.1875),
        "binarizer_offset": jnp.clip(jax.random.uniform(keys[7], (BITS,), jnp.float32, -1.0, 1.0), -1.0, 1.0),
    }


epsilon = 1e-06

def rms_scale(values):
    return lax.rsqrt(lax.optimization_barrier(jnp.mean(values * values, axis=-1, keepdims=True)) + epsilon)

def split_subspaces(combined_subspaces, scales, channel_extent):
    token_count = combined_subspaces.shape[0]
    pieces = combined_subspaces.reshape(token_count, 3, scales.shape[0], channel_extent).astype(jnp.float32)
    asking_tensor = pieces[:, 0] * rms_scale(pieces[:, 0]) * (scales[:, None] / math.sqrt(channel_extent))
    rescaled_lookups = pieces[:, 1] * rms_scale(pieces[:, 1])
    return (asking_tensor.astype(jnp.bfloat16), rescaled_lookups.astype(jnp.bfloat16), pieces[:, 2].astype(jnp.bfloat16))

def bundled_mixing_block(bundled_tokens, picture_label_column, prenorm_multiplier, triple_projector, logit_scaling, final_projector, binarizer_projector, binarizer_offset):
    wide_pack = bundled_tokens.astype(jnp.float32)
    normed = (wide_pack * rms_scale(wide_pack) * prenorm_multiplier).astype(jnp.bfloat16)
    combined_subspaces = jnp.dot(normed, triple_projector, preferred_element_type=jnp.float32).astype(jnp.bfloat16)
    asking_tensor, rescaled_lookups, surviving_contents = split_subspaces(combined_subspaces, logit_scaling, CHANNEL_COUNT)
    same_image = picture_label_column[:, None] == picture_label_column[None, :]

    def one_head(contraction_operands):
        query_head, key_head, value_head = contraction_operands
        scores = jnp.dot(query_head, key_head.T, preferred_element_type=jnp.float32)
        masked = jnp.where(same_image, scores, -1e+30)
        highest = lax.optimization_barrier(jnp.max(masked, axis=-1, keepdims=True))
        probs = jnp.where(same_image, jnp.exp(scores - highest), 0.0)
        weights = probs.astype(jnp.bfloat16)
        summed = jnp.dot(weights, value_head, preferred_element_type=jnp.float32)
        return summed / lax.optimization_barrier(jnp.sum(probs, axis=-1, keepdims=True))
    attended = lax.map(one_head, (jnp.swapaxes(asking_tensor, 0, 1), jnp.swapaxes(rescaled_lookups, 0, 1), jnp.swapaxes(surviving_contents, 0, 1)))
    attention = jnp.swapaxes(attended, 0, 1).reshape(SEQ, D).astype(jnp.bfloat16)
    hidden_state = wide_pack + jnp.dot(attention, final_projector, preferred_element_type=jnp.float32)
    mixed = hidden_state.astype(jnp.bfloat16)
    logits = jnp.dot(mixed, binarizer_projector, preferred_element_type=jnp.float32) + binarizer_offset
    return (mixed, jax.nn.sigmoid(4.0 * logits))

def reference(residual_tiles, picture_label_tile, prenorm_multiplier, triple_projector, logit_scaling, final_projector, binarizer_projector, binarizer_offset):

    def one_pack(contraction_operands):
        return bundled_mixing_block(contraction_operands[0], contraction_operands[1], prenorm_multiplier, triple_projector, logit_scaling, final_projector, binarizer_projector, binarizer_offset)
    mixed, bit_probs = lax.map(one_pack, (residual_tiles, picture_label_tile))
    marginal = lax.optimization_barrier(jnp.sum(bit_probs, axis=(0, 1))) / (PACKS * SEQ)
    code_entropy = -(marginal * jnp.log(marginal) + (1.0 - marginal) * jnp.log(1.0 - marginal))
    bit_codes = jnp.swapaxes(bit_probs - marginal, 1, 2)
    return (mixed, bit_codes, code_entropy)
```

```python
import functools
import math

import jax
import jax.numpy as jnp
from jax import lax
from jax.experimental import pallas as pl
from jax.experimental.pallas import tpu as pltpu
from jax.sharding import Mesh
from jax.sharding import PartitionSpec as P

SEQ = ("seq_0", "seq_1")
DP = ("dp_0", "dp_1")
ALL = ("dp_0", "dp_1", "seq_0", "seq_1")

EPS = 1e-06
EXCLUDED = -32768.0
KEYS = 512
ROWS = 256
SAFE = 8.0
LIMIT = 60 * 1024 * 1024
F32 = jnp.float32
BF16 = jnp.bfloat16


def params():
    return pltpu.CompilerParams(vmem_limit_bytes=LIMIT)


def vmem():
    return pl.BlockSpec(memory_space=pltpu.VMEM)


def smem():
    return pl.BlockSpec(memory_space=pltpu.SMEM)


def copy_for_each(x, axis):
    length = lax.axis_size(axis)
    return lax.all_to_all(jnp.broadcast_to(x[None], (length, *x.shape)), axis, 0, 0, tiled=True)


def any_space():
    return pl.BlockSpec(memory_space=pl.ANY)


def layer_kernel(at, scale, gain, *refs):
    pieces, shards, out = refs[:8], refs[8], refs[9]
    held, weights, normed, labels, queries, keys, values, total, even, odd, table, sems = refs[10:]
    core, chip = at[0], at[1]
    rows = ROWS
    arrivals = [
        pltpu.make_async_copy(pieces[i], held.at[i // 2, i % 2], sems.at[i]) for i in range(8)
    ]
    for i in range(4):
        copy = pltpu.make_async_copy(shards.at[i], weights.at[:, i], sems.at[8 + i])
        copy.start()
        arrivals.append(copy)
    for copy in arrivals[:8]:
        copy.start()
    for copy in arrivals[8:]:
        copy.wait()
    width, head = held.shape[3], 64
    matrix = weights[...].reshape(width, 384)
    lane = lax.broadcasted_iota(jnp.int32, (rows, 128), 1)
    spot = lax.broadcasted_iota(jnp.int32, (head, rows), 0)
    for pair in range(4):
        step = (0, 1, 3, 2)[pair]
        for side in range(2):
            arrivals[2 * pair + side].wait()
            wide = held[pair, side, 0:rows].astype(F32)
            inv = lax.rsqrt(jnp.mean(wide * wide, axis=-1, keepdims=True) + EPS)
            normed[side * rows : (side + 1) * rows] = (wide * inv * gain[...]).astype(BF16)
        both = jnp.dot(normed[...], matrix, preferred_element_type=F32).astype(BF16).astype(F32)
        for side in range(2):
            part = core if side == 0 else 1 - core
            block = 2 * lax.rem(chip + step, 4) + part
            start = pl.multiple_of(block * rows, rows)
            joined = both[side * rows : (side + 1) * rows]
            ids = held[pair, side, rows : rows + 8, 0:rows].astype(F32)[0:1].astype(jnp.int32)
            labels[pl.ds(block, 1), :] = ids
            same = spot == ids
            bars = jnp.where(same, 0.0, EXCLUDED).astype(F32)
            query = joined[:, 0:128].T
            key = joined[:, 128:256].T
            marks = jnp.where(same, 1.0, 0.0).astype(BF16)
            for h in range(2):
                one = query[h * head : (h + 1) * head]
                inv = lax.rsqrt(jnp.mean(one * one, axis=0, keepdims=True) + EPS)
                queries[h, pl.ds(start, rows), :] = (
                    jnp.concatenate([one * inv * scale[h], bars], axis=0).T.astype(BF16)
                )
                one = key[h * head : (h + 1) * head]
                inv = lax.rsqrt(jnp.mean(one * one, axis=0, keepdims=True) + EPS)
                keys[h, 0:head, pl.ds(start, rows)] = (one * inv).astype(BF16)
                keys[h, head : 2 * head, pl.ds(start, rows)] = marks
            value = joined[:, 256:384]
            values[0, pl.ds(start, rows), :] = jnp.where(lane < head, value, 1.0).astype(BF16)
            values[1, pl.ds(start, rows), :] = jnp.where(
                lane < head, pltpu.roll(value, head, 1), 1.0
            ).astype(BF16)

    every = labels[...]
    first, last = every[:, 0:1], every[:, rows - 1 : rows]
    below = jnp.zeros((8, rows), jnp.int32)
    upto = jnp.zeros((8, rows), jnp.int32)
    for b in range(8):
        below += (every[b : b + 1] < first).astype(jnp.int32)
        upto += (every[b : b + 1] <= last).astype(jnp.int32)
    low = jnp.sum(below, axis=1, keepdims=True)
    high = jnp.sum(upto, axis=1, keepdims=True)
    low = low & -128
    counts = lax.shift_right_logical(high - low + (KEYS - 1), 9)
    low = jnp.minimum(low, 2048 - counts * KEYS)
    lows = [low[b, 0] for b in range(8)]
    counts = [counts[b, 0] for b in range(8)]
    total[...] = jnp.zeros(total.shape, F32)

    pairs = jnp.int32(0)
    for b in range(8):

        def note(s, pairs, b=b):
            table[0, pairs] = jnp.int32(b * rows)
            table[1, pairs] = lows[b] + s * KEYS
            return pairs + 1

        pairs = lax.fori_loop(0, counts[b], note, pairs)
    for spare in range(2):
        table[0, pairs + spare] = jnp.int32(8 * rows)
        table[1, pairs + spare] = jnp.int32(0)

    def score(j, into):
        row = pl.multiple_of(table[0, j], rows)
        key = pl.multiple_of(table[1, j], 128)
        for h in range(2):
            into[h] = jnp.dot(
                queries[h, pl.ds(row, rows), :],
                keys[h, :, pl.ds(key, KEYS)],
                preferred_element_type=F32,
            )

    def absorb(j, source):
        row = pl.multiple_of(table[0, j], rows)
        key = pl.multiple_of(table[1, j], 128)
        for h in range(2):
            total[h, pl.ds(row, rows), :] += jnp.dot(
                jnp.exp(source[h]).astype(BF16),
                values[h, pl.ds(key, KEYS), :],
                preferred_element_type=F32,
            )

    small = jnp.maximum(scale[0], scale[1]) * 8.0 <= SAFE

    @pl.when(small)
    def _():
        score(0, even)

        def twice(j, carry):
            score(2 * j + 1, odd)
            absorb(2 * j, even)
            score(2 * j + 2, even)
            absorb(2 * j + 1, odd)
            return carry

        lax.fori_loop(0, (pairs + 1) // 2, twice, 0)

    @pl.when(jnp.logical_not(small))
    def _():
        for b in range(8):
            own = pl.ds(b * rows, rows)
            for h in range(2):

                def scores(j, b=b, h=h, own=own):
                    key = pl.multiple_of(lows[b] + j * KEYS, 128)
                    return key, jnp.dot(
                        queries[h, own, :], keys[h, :, pl.ds(key, KEYS)], preferred_element_type=F32
                    )

                def top(j, most, scores=scores):
                    return jnp.maximum(most, jnp.max(scores(j)[1], axis=-1, keepdims=True))

                largest = lax.fori_loop(
                    0, counts[b], top, jnp.full((rows, 1), 2.0 * EXCLUDED, F32)
                )

                def gather(j, carry, h=h, own=own, scores=scores, largest=largest):
                    key, found = scores(j)
                    total[h, own, :] += jnp.dot(
                        jnp.exp(found - largest).astype(BF16),
                        values[h, pl.ds(key, KEYS), :],
                        preferred_element_type=F32,
                    )
                    return carry

                lax.fori_loop(0, counts[b], gather, 0)

    for b in range(8):
        own = slice(b * rows, (b + 1) * rows)
        left, right = total[0, own, :], total[1, own, :]
        over = jnp.where(lane < head, left, pltpu.roll(right, head, 1))
        under = jnp.where(lane < head, pltpu.roll(left, head, 1), right)
        out[b] = (over / under).astype(BF16)


def layer(at, scale, gain, pieces, shard):
    total = 8 * ROWS
    return pl.pallas_call(
        layer_kernel,
        in_specs=[smem(), smem(), vmem()] + [any_space()] * 9,
        out_specs=vmem(),
        out_shape=jax.ShapeDtypeStruct((8, ROWS, 128), BF16),
        scratch_shapes=[
            pltpu.VMEM((4, 2, *pieces[0].shape), BF16),
            pltpu.VMEM((8, 4, 32, 384), BF16),
            pltpu.VMEM((2 * ROWS, pieces[0].shape[1]), BF16),
            pltpu.VMEM((8, ROWS), jnp.int32),
            pltpu.VMEM((2, total + ROWS, 128), BF16),
            pltpu.VMEM((2, 128, total), BF16),
            pltpu.VMEM((2, total, 128), BF16),
            pltpu.VMEM((2, total + ROWS, 128), F32),
            pltpu.VMEM((2, ROWS, KEYS), F32),
            pltpu.VMEM((2, ROWS, KEYS), F32),
            pltpu.SMEM((2, 48), jnp.int32),
            pltpu.SemaphoreType.DMA((12,)),
        ],
        compiler_params=params(),
        name="layer",
    )(at, scale, gain, *pieces, shard)


def finish_kernel(at, pieces, *refs):
    shards, (rows, bits, offset, mixed, probs, sums, weights, joined, sems) = refs[:8], refs[8:]
    copies = []
    for i in range(8):
        part = at[0] if i < 4 else 1 - at[0]
        place = lax.rem(at[2] + (0, 2, 1, 3)[i % 4], 4)
        copies.append(pltpu.make_async_copy(shards[i], weights.at[part, :, place], sems.at[i]))
        copies[i].start()
    for source in range(8):
        joined[:, source * 128 : (source + 1) * 128] = pieces[source]
    for copy in copies:
        copy.wait()
    for part in range(2):
        columns = slice(part * 512, part * 512 + 512)
        moved = jnp.dot(
            joined[...], weights[part].reshape(1024, 512), preferred_element_type=F32
        )
        mixed[:, columns] = (rows[:, columns].astype(F32) + moved).astype(BF16)
    logits = lax.dot_general(
        bits[...], mixed[...], (((1,), (1,)), ((), ())), preferred_element_type=F32
    )
    chance = jax.nn.sigmoid(4.0 * (logits + offset[...]))
    probs[...] = chance
    row = lax.dot_general(
        jnp.ones((8, chance.shape[1]), F32),
        chance,
        (((1,), (1,)), ((), ())),
        preferred_element_type=F32,
        precision=lax.Precision.HIGHEST,
    )
    sums[...] = row[0:1]


def finish(at, pieces, shards, rows, bits, offset):
    count = rows.shape[0]
    return pl.pallas_call(
        finish_kernel,
        in_specs=[smem(), vmem()] + [any_space()] * 8 + [vmem()] * 3,
        out_specs=[vmem()] * 3,
        out_shape=[
            jax.ShapeDtypeStruct(rows.shape, BF16),
            jax.ShapeDtypeStruct((bits.shape[0], count), F32),
            jax.ShapeDtypeStruct((1, bits.shape[0]), F32),
        ],
        scratch_shapes=[
            pltpu.VMEM((2, 8, 4, 32, 512), BF16),
            pltpu.VMEM((count, 1024), BF16),
            pltpu.SemaphoreType.DMA((8,)),
        ],
        compiler_params=params(),
        name="finish",
    )(at, pieces, *shards, rows, bits, offset)


def on_device(
    residual_tiles,
    picture_label_tile,
    prenorm_multiplier,
    triple_projector,
    logit_scaling,
    final_projector,
    binarizer_projector,
    binarizer_offset,
):
    rows = residual_tiles[0]
    count, width = rows.shape
    core = lax.axis_index("seq_1")
    member = lax.axis_index(SEQ)
    at = jnp.stack([core, lax.axis_index("seq_0"), lax.axis_index("dp_1")]).astype(jnp.int32)

    def from_step(x, k, axis="seq_0"):
        length = lax.axis_size(axis)
        return lax.ppermute(x, axis, [(i, (i - k) % length) for i in range(length)])

    def from_other_core(x):
        return lax.ppermute(x, "seq_1", [(0, 1), (1, 0)])

    marked = jnp.pad(picture_label_tile.astype(BF16), ((0, 15), (0, width - count)))
    load = jnp.concatenate([rows, marked], axis=0)
    near = [load] + [from_step(load, k) for k in (1, 3, 2)]
    pieces = [x for own in near for x in (own, from_other_core(own))]

    owned = jnp.concatenate(
        [
            lax.dynamic_slice_in_dim(triple_projector, member * 128 + 1024 * i, 128, 1)
            for i in range(3)
        ]
        + [lax.dynamic_slice_in_dim(final_projector, core * 512, 512, 1)],
        axis=1,
    )
    owned = copy_for_each(owned, "dp_0")
    shard, mixing = owned[:, :, :384], owned[:, :, 384:]
    shard = copy_for_each(shard, "dp_1")
    mixing, _ = lax.optimization_barrier((mixing, shard))
    mixings = [mixing] + [from_step(mixing, k, "dp_1") for k in (2, 1, 3)]

    scale = lax.dynamic_slice_in_dim(logit_scaling, member * 2, 2, 0) / math.sqrt(64)
    attended = layer(at, scale, prenorm_multiplier[None], pieces, shard)
    mixings, attended = lax.optimization_barrier((mixings, attended))
    mixings = mixings + [from_other_core(m) for m in mixings]
    attended = lax.all_to_all(attended, SEQ, 0, 0, tiled=True)
    mixed, probs, sums = finish(
        at,
        attended,
        mixings,
        rows,
        binarizer_projector.T,
        binarizer_offset[:, None],
    )
    sums = sums + from_other_core(sums)
    sums = copy_for_each(sums, ("dp_0", "dp_1", "seq_0"))
    marginal = jnp.sum(sums, axis=(0, 1)) / (count * lax.axis_size(ALL))
    code_entropy = -(marginal * jnp.log(marginal) + (1.0 - marginal) * jnp.log(1.0 - marginal))
    bit_codes = (probs - marginal[:, None])[None]
    return (mixed[None], bit_codes, code_entropy)


def solution(mesh):
    finer = Mesh(mesh.devices.reshape(8, 4, 4, 2), ("dp_0", "dp_1", "seq_0", "seq_1"))
    placed = (P(DP, SEQ, None), P(DP, SEQ), P(), P(DP, None), P(), P(DP, None), P(), P())
    return jax.shard_map(
        on_device,
        mesh=finer,
        in_specs=placed,
        out_specs=(P(DP, SEQ, None), P(DP, None, SEQ), P()),
        check_vma=False,
    )
```

```python
import functools
import math

import jax
import jax.numpy as jnp
from jax import lax
from jax.experimental import pallas as pl
from jax.experimental.pallas import tpu as pltpu
from jax.sharding import Mesh
from jax.sharding import PartitionSpec as P

SEQ = ("seq_0", "seq_1")
DP = ("dp_0", "dp_1")
ALL = ("dp_0", "dp_1", "seq_0", "seq_1")

EPS = 1e-06
EXCLUDED = -32768.0
KEYS = 512
ROWS = 256
SAFE = 8.0
LIMIT = 60 * 1024 * 1024
F32 = jnp.float32
BF16 = jnp.bfloat16


def params():
    return pltpu.CompilerParams(vmem_limit_bytes=LIMIT)


def vmem():
    return pl.BlockSpec(memory_space=pltpu.VMEM)


def smem():
    return pl.BlockSpec(memory_space=pltpu.SMEM)


def copy_for_each(x, axis):
    length = lax.axis_size(axis)
    return lax.all_to_all(jnp.broadcast_to(x[None], (length, *x.shape)), axis, 0, 0, tiled=True)


def any_space():
    return pl.BlockSpec(memory_space=pl.ANY)


def layer_kernel(scales, gain, *refs):
    pieces, shards, out = refs[:8], refs[8], refs[9]
    held, weights, normed, labels, queries, keys, values, total, even, odd, table, sems = refs[10:]
    core, chip = lax.axis_index("seq_1"), lax.axis_index("seq_0")
    first = (2 * chip + core) * 2
    scale = [scales[first] / math.sqrt(64), scales[first + 1] / math.sqrt(64)]
    rows = ROWS
    arrivals = [
        pltpu.make_async_copy(pieces[i], held.at[i // 2, i % 2], sems.at[i]) for i in range(8)
    ]
    matrix = pltpu.make_async_copy(shards.at[:, pl.ds(0, 384)], weights, sems.at[8])
    matrix.start()
    for copy in arrivals:
        copy.start()
    matrix.wait()
    head = 64
    lane = lax.broadcasted_iota(jnp.int32, (rows, 128), 1)
    spot = lax.broadcasted_iota(jnp.int32, (head, rows), 0)
    for pair in range(4):
        step = (0, 1, 3, 2)[pair]
        for side in range(2):
            arrivals[2 * pair + side].wait()
            wide = held[pair, side, 0:rows].astype(F32)
            inv = lax.rsqrt(jnp.mean(wide * wide, axis=-1, keepdims=True) + EPS)
            normed[side * rows : (side + 1) * rows] = (wide * inv * gain[...]).astype(BF16)
        both = jnp.dot(normed[...], weights[...], preferred_element_type=F32).astype(BF16).astype(F32)
        for side in range(2):
            part = core if side == 0 else 1 - core
            block = 2 * lax.rem(chip + step, 4) + part
            start = pl.multiple_of(block * rows, rows)
            joined = both[side * rows : (side + 1) * rows]
            ids = held[pair, side, rows : rows + 8, 0:rows].astype(F32)[0:1].astype(jnp.int32)
            labels[pl.ds(block, 1), :] = ids
            same = spot == ids
            bars = jnp.where(same, 0.0, EXCLUDED).astype(F32)
            query = joined[:, 0:128].T
            key = joined[:, 128:256].T
            marks = jnp.where(same, 1.0, 0.0).astype(BF16)
            for h in range(2):
                one = query[h * head : (h + 1) * head]
                inv = lax.rsqrt(jnp.mean(one * one, axis=0, keepdims=True) + EPS)
                queries[h, pl.ds(start, rows), :] = (
                    jnp.concatenate([one * inv * scale[h], bars], axis=0).T.astype(BF16)
                )
                one = key[h * head : (h + 1) * head]
                inv = lax.rsqrt(jnp.mean(one * one, axis=0, keepdims=True) + EPS)
                keys[h, 0:head, pl.ds(start, rows)] = (one * inv).astype(BF16)
                keys[h, head : 2 * head, pl.ds(start, rows)] = marks
            value = joined[:, 256:384]
            values[0, pl.ds(start, rows), :] = jnp.where(lane < head, value, 1.0).astype(BF16)
            values[1, pl.ds(start, rows), :] = jnp.where(
                lane < head, pltpu.roll(value, head, 1), 1.0
            ).astype(BF16)

    every = labels[...]
    opening, closing = every[:, 0:1], every[:, rows - 1 : rows]
    below = jnp.zeros((8, rows), jnp.int32)
    upto = jnp.zeros((8, rows), jnp.int32)
    for b in range(8):
        below += (every[b : b + 1] < opening).astype(jnp.int32)
        upto += (every[b : b + 1] <= closing).astype(jnp.int32)
    low = jnp.sum(below, axis=1, keepdims=True)
    high = jnp.sum(upto, axis=1, keepdims=True)
    low = low & -128
    counts = lax.shift_right_logical(high - low + (KEYS - 1), 9)
    low = jnp.minimum(low, 2048 - counts * KEYS)
    lows = [low[b, 0] for b in range(8)]
    counts = [counts[b, 0] for b in range(8)]
    total[...] = jnp.zeros(total.shape, F32)

    pairs = jnp.int32(0)
    for b in range(8):

        def note(s, pairs, b=b):
            table[0, pairs] = jnp.int32(b * rows)
            table[1, pairs] = lows[b] + s * KEYS
            return pairs + 1

        pairs = lax.fori_loop(0, counts[b], note, pairs)
    for spare in range(2):
        table[0, pairs + spare] = jnp.int32(8 * rows)
        table[1, pairs + spare] = jnp.int32(0)

    def score(j, into):
        row = pl.multiple_of(table[0, j], rows)
        key = pl.multiple_of(table[1, j], 128)
        for h in range(2):
            into[h] = jnp.dot(
                queries[h, pl.ds(row, rows), :],
                keys[h, :, pl.ds(key, KEYS)],
                preferred_element_type=F32,
            )

    def absorb(j, source):
        row = pl.multiple_of(table[0, j], rows)
        key = pl.multiple_of(table[1, j], 128)
        for h in range(2):
            total[h, pl.ds(row, rows), :] += jnp.dot(
                jnp.exp(source[h]).astype(BF16),
                values[h, pl.ds(key, KEYS), :],
                preferred_element_type=F32,
            )

    small = jnp.maximum(scales[first], scales[first + 1]) <= SAFE

    @pl.when(small)
    def _():
        score(0, even)

        def twice(j, carry):
            score(2 * j + 1, odd)
            absorb(2 * j, even)
            score(2 * j + 2, even)
            absorb(2 * j + 1, odd)
            return carry

        lax.fori_loop(0, (pairs + 1) // 2, twice, 0)

    @pl.when(jnp.logical_not(small))
    def _():
        for b in range(8):
            own = pl.ds(b * rows, rows)
            for h in range(2):

                def scores(j, b=b, h=h, own=own):
                    key = pl.multiple_of(lows[b] + j * KEYS, 128)
                    return key, jnp.dot(
                        queries[h, own, :], keys[h, :, pl.ds(key, KEYS)], preferred_element_type=F32
                    )

                def top(j, most, scores=scores):
                    return jnp.maximum(most, jnp.max(scores(j)[1], axis=-1, keepdims=True))

                largest = lax.fori_loop(
                    0, counts[b], top, jnp.full((rows, 1), 2.0 * EXCLUDED, F32)
                )

                def gather(j, carry, h=h, own=own, scores=scores, largest=largest):
                    key, found = scores(j)
                    total[h, own, :] += jnp.dot(
                        jnp.exp(found - largest).astype(BF16),
                        values[h, pl.ds(key, KEYS), :],
                        preferred_element_type=F32,
                    )
                    return carry

                lax.fori_loop(0, counts[b], gather, 0)

    for b in range(8):
        own = slice(b * rows, (b + 1) * rows)
        left, right = total[0, own, :], total[1, own, :]
        over = jnp.where(lane < head, left, pltpu.roll(right, head, 1))
        under = jnp.where(lane < head, pltpu.roll(left, head, 1), right)
        out[b] = (over / under).astype(BF16)


def layer(scales, gain, pieces, shard):
    total = 8 * ROWS
    return pl.pallas_call(
        layer_kernel,
        in_specs=[smem(), vmem()] + [any_space()] * 9,
        out_specs=vmem(),
        out_shape=jax.ShapeDtypeStruct((8, ROWS, 128), BF16),
        scratch_shapes=[
            pltpu.VMEM((4, 2, *pieces[0].shape), BF16),
            pltpu.VMEM((shard.shape[0], 384), BF16),
            pltpu.VMEM((2 * ROWS, pieces[0].shape[1]), BF16),
            pltpu.VMEM((8, ROWS), jnp.int32),
            pltpu.VMEM((2, total + ROWS, 128), BF16),
            pltpu.VMEM((2, 128, total), BF16),
            pltpu.VMEM((2, total, 128), BF16),
            pltpu.VMEM((2, total + ROWS, 128), F32),
            pltpu.VMEM((2, ROWS, KEYS), F32),
            pltpu.VMEM((2, ROWS, KEYS), F32),
            pltpu.SMEM((2, 48), jnp.int32),
            pltpu.SemaphoreType.DMA((9,)),
        ],
        compiler_params=params(),
        name="layer",
    )(scales, gain, *pieces, shard)


def finish_kernel(pieces, *refs):
    shards, (rows, bits, offset, mixed, probs, sums, weights, joined, sems) = refs[:8], refs[8:]
    core, chip = lax.axis_index("seq_1"), lax.axis_index("seq_0")
    copies = []
    for i in range(8):
        block = 2 * lax.rem(chip + i % 4, 4) + (core if i < 4 else 1 - core)
        columns = pl.ds(pl.multiple_of(block * 128, 128), 128)
        copies.append(pltpu.make_async_copy(shards[i], weights.at[:, columns], sems.at[i]))
        copies[i].start()
    for source in range(8):
        joined[:, source * 128 : (source + 1) * 128] = pieces[source]
    for copy in copies:
        copy.wait()
    moved = jnp.dot(joined[...], weights[...], preferred_element_type=F32)
    mixed[...] = (rows[...].astype(F32) + moved).astype(BF16)
    logits = lax.dot_general(
        bits[...], mixed[...], (((1,), (1,)), ((), ())), preferred_element_type=F32
    )
    chance = jax.nn.sigmoid(4.0 * (logits + offset[...]))
    for b in range(chance.shape[0]):
        probs[b] = chance[b : b + 1]
    row = lax.dot_general(
        jnp.ones((8, chance.shape[1]), F32),
        chance,
        (((1,), (1,)), ((), ())),
        preferred_element_type=F32,
        precision=lax.Precision.HIGHEST,
    )
    sums[...] = row[0:1]


def finish(pieces, shards, rows, bits, offset):
    count = rows.shape[0]
    return pl.pallas_call(
        finish_kernel,
        in_specs=[vmem()] + [any_space()] * 8 + [vmem()] * 3,
        out_specs=[vmem()] * 3,
        out_shape=[
            jax.ShapeDtypeStruct(rows.shape, BF16),
            jax.ShapeDtypeStruct((bits.shape[0], 1, count), F32),
            jax.ShapeDtypeStruct((1, bits.shape[0]), F32),
        ],
        scratch_shapes=[
            pltpu.VMEM((1024, 1024), BF16),
            pltpu.VMEM((count, 1024), BF16),
            pltpu.SemaphoreType.DMA((8,)),
        ],
        compiler_params=params(),
        name="finish",
    )(pieces, *shards, rows, bits, offset)


def on_device(
    residual_tiles,
    picture_label_tile,
    prenorm_multiplier,
    triple_projector,
    logit_scaling,
    final_projector,
    binarizer_projector,
    binarizer_offset,
):
    rows = residual_tiles[0]
    count, width = rows.shape
    member = lax.axis_index(SEQ)
    def from_step(x, k, axis="seq_0"):
        length = lax.axis_size(axis)
        return lax.ppermute(x, axis, [(i, (i - k) % length) for i in range(length)])

    def from_other_core(x):
        return lax.ppermute(x, "seq_1", [(0, 1), (1, 0)])

    marked = jnp.pad(picture_label_tile.astype(BF16), ((0, 15), (0, width - count)))
    load = jnp.concatenate([rows, marked], axis=0)
    near = [load] + [from_step(load, k) for k in (1, 3, 2)]
    pieces = [x for own in near for x in (own, from_other_core(own))]

    owned = jnp.concatenate(
        [
            lax.dynamic_slice_in_dim(triple_projector, member * 128 + 1024 * i, 128, 1)
            for i in range(3)
        ]
        + [lax.dynamic_slice_in_dim(final_projector, member * 128, 128, 1)],
        axis=1,
    )
    shard = copy_for_each(owned, DP).reshape(width, 512)
    mixing, _ = lax.optimization_barrier((shard[:, 384:], near))
    mixings = [mixing] + [from_step(mixing, k) for k in (1, 2, 3)]

    attended = layer(logit_scaling, prenorm_multiplier[None], pieces, shard)
    mixings, attended = lax.optimization_barrier((mixings, attended))
    mixings = mixings + [from_other_core(m) for m in mixings]
    attended = lax.all_to_all(attended, SEQ, 0, 0, tiled=True)
    mixed, probs, sums = finish(
        attended,
        mixings,
        rows,
        binarizer_projector.T,
        binarizer_offset[:, None],
    )
    sums = sums + from_other_core(sums)
    sums = copy_for_each(sums, ("dp_0", "dp_1", "seq_0"))
    marginal = jnp.sum(sums, axis=(0, 1)) / (count * lax.axis_size(ALL))
    code_entropy = -(marginal * jnp.log(marginal) + (1.0 - marginal) * jnp.log(1.0 - marginal))
    bit_codes = jnp.swapaxes(probs - marginal[:, None, None], 0, 1)
    return (mixed[None], bit_codes, code_entropy)


def solution(mesh):
    finer = Mesh(mesh.devices.reshape(8, 4, 4, 2), ("dp_0", "dp_1", "seq_0", "seq_1"))
    placed = (P(DP, SEQ, None), P(DP, SEQ), P(), P(DP, None), P(), P(DP, None), P(), P())
    return jax.shard_map(
        on_device,
        mesh=finer,
        in_specs=placed,
        out_specs=(P(DP, SEQ, None), P(DP, None, SEQ), P()),
        check_vma=False,
    )
```

```python
import functools
import math

import jax
import jax.numpy as jnp
from jax import lax
from jax.experimental import pallas as pl
from jax.experimental.pallas import tpu as pltpu
from jax.sharding import Mesh
from jax.sharding import PartitionSpec as P

SEQ = ("seq_0", "seq_1")
DP = ("dp_0", "dp_1")
ALL = ("dp_0", "dp_1", "seq_0", "seq_1")

EPS = 1e-06
EXCLUDED = -32768.0
KEYS = 512
ROWS = 256
SAFE = 8.0
LIMIT = 28 * 1024 * 1024
F32 = jnp.float32
BF16 = jnp.bfloat16


def params():
    return pltpu.CompilerParams(vmem_limit_bytes=LIMIT)


def vmem():
    return pl.BlockSpec(memory_space=pltpu.VMEM)


def smem():
    return pl.BlockSpec(memory_space=pltpu.SMEM)


def in_vmem(tree):
    return jax.tree.map(lambda x: pltpu.with_memory_space_constraint(x, pltpu.VMEM), tree)


def copy_for_each(x, axis):
    length = lax.axis_size(axis)
    return lax.all_to_all(jnp.broadcast_to(x[None], (length, *x.shape)), axis, 0, 0, tiled=True)


def layer_kernel(scales, gain, *refs):
    pieces, shards, out = refs[:8], refs[8], refs[9]
    weights, normed, labels, queries, keys, values, total, even, odd, table = refs[10:]
    core, chip = lax.axis_index("seq_1"), lax.axis_index("seq_0")
    first = (2 * chip + core) * 2
    scale = [scales[first] / math.sqrt(64), scales[first + 1] / math.sqrt(64)]
    rows = ROWS
    for i in range(4):
        weights[:, i] = shards[i]
    head = 64
    matrix = weights[...].reshape(normed.shape[1], 384)
    lane = lax.broadcasted_iota(jnp.int32, (rows, 128), 1)
    spot = lax.broadcasted_iota(jnp.int32, (head, rows), 0)
    for pair in range(4):
        step = (0, 1, 3, 2)[pair]
        for side in range(2):
            wide = pieces[2 * pair + side][0:rows].astype(F32)
            inv = lax.rsqrt(jnp.mean(wide * wide, axis=-1, keepdims=True) + EPS)
            normed[side * rows : (side + 1) * rows] = (wide * inv * gain[...]).astype(BF16)
        both = jnp.dot(normed[...], matrix, preferred_element_type=F32).astype(BF16).astype(F32)
        for side in range(2):
            part = core if side == 0 else 1 - core
            block = 2 * lax.rem(chip + step, 4) + part
            start = pl.multiple_of(block * rows, rows)
            joined = both[side * rows : (side + 1) * rows]
            ids = pieces[2 * pair + side][rows : rows + 8, 0:rows].astype(F32)[0:1].astype(jnp.int32)
            labels[pl.ds(block, 1), :] = ids
            same = spot == ids
            bars = jnp.where(same, 0.0, EXCLUDED).astype(F32)
            query = joined[:, 0:128].T
            key = joined[:, 128:256].T
            marks = jnp.where(same, 1.0, 0.0).astype(BF16)
            for h in range(2):
                one = query[h * head : (h + 1) * head]
                inv = lax.rsqrt(jnp.mean(one * one, axis=0, keepdims=True) + EPS)
                queries[h, pl.ds(start, rows), :] = (
                    jnp.concatenate([one * inv * scale[h], bars], axis=0).T.astype(BF16)
                )
                one = key[h * head : (h + 1) * head]
                inv = lax.rsqrt(jnp.mean(one * one, axis=0, keepdims=True) + EPS)
                keys[h, 0:head, pl.ds(start, rows)] = (one * inv).astype(BF16)
                keys[h, head : 2 * head, pl.ds(start, rows)] = marks
            value = joined[:, 256:384]
            values[0, pl.ds(start, rows), :] = jnp.where(lane < head, value, 1.0).astype(BF16)
            values[1, pl.ds(start, rows), :] = jnp.where(
                lane < head, pltpu.roll(value, head, 1), 1.0
            ).astype(BF16)

    every = labels[...]
    opening, closing = every[:, 0:1], every[:, rows - 1 : rows]
    below = jnp.zeros((8, rows), jnp.int32)
    upto = jnp.zeros((8, rows), jnp.int32)
    for b in range(8):
        below += (every[b : b + 1] < opening).astype(jnp.int32)
        upto += (every[b : b + 1] <= closing).astype(jnp.int32)
    low = jnp.sum(below, axis=1, keepdims=True)
    high = jnp.sum(upto, axis=1, keepdims=True)
    low = low & -128
    counts = lax.shift_right_logical(high - low + (KEYS - 1), 9)
    low = jnp.minimum(low, 2048 - counts * KEYS)
    lows = [low[b, 0] for b in range(8)]
    counts = [counts[b, 0] for b in range(8)]
    total[...] = jnp.zeros(total.shape, F32)

    pairs = jnp.int32(0)
    for b in range(8):

        def note(s, pairs, b=b):
            table[0, pairs] = jnp.int32(b * rows)
            table[1, pairs] = lows[b] + s * KEYS
            return pairs + 1

        pairs = lax.fori_loop(0, counts[b], note, pairs)
    for spare in range(2):
        table[0, pairs + spare] = jnp.int32(8 * rows)
        table[1, pairs + spare] = jnp.int32(0)

    def score(j, into):
        row = pl.multiple_of(table[0, j], rows)
        key = pl.multiple_of(table[1, j], 128)
        for h in range(2):
            into[h] = jnp.dot(
                queries[h, pl.ds(row, rows), :],
                keys[h, :, pl.ds(key, KEYS)],
                preferred_element_type=F32,
            )

    def absorb(j, source):
        row = pl.multiple_of(table[0, j], rows)
        key = pl.multiple_of(table[1, j], 128)
        for h in range(2):
            total[h, pl.ds(row, rows), :] += jnp.dot(
                jnp.exp(source[h]).astype(BF16),
                values[h, pl.ds(key, KEYS), :],
                preferred_element_type=F32,
            )

    small = jnp.maximum(scales[first], scales[first + 1]) <= SAFE

    @pl.when(small)
    def _():
        score(0, even)

        def twice(j, carry):
            score(2 * j + 1, odd)
            absorb(2 * j, even)
            score(2 * j + 2, even)
            absorb(2 * j + 1, odd)
            return carry

        lax.fori_loop(0, (pairs + 1) // 2, twice, 0)

    @pl.when(jnp.logical_not(small))
    def _():
        for b in range(8):
            own = pl.ds(b * rows, rows)
            for h in range(2):

                def scores(j, b=b, h=h, own=own):
                    key = pl.multiple_of(lows[b] + j * KEYS, 128)
                    return key, jnp.dot(
                        queries[h, own, :], keys[h, :, pl.ds(key, KEYS)], preferred_element_type=F32
                    )

                def top(j, most, scores=scores):
                    return jnp.maximum(most, jnp.max(scores(j)[1], axis=-1, keepdims=True))

                largest = lax.fori_loop(
                    0, counts[b], top, jnp.full((rows, 1), 2.0 * EXCLUDED, F32)
                )

                def gather(j, carry, h=h, own=own, scores=scores, largest=largest):
                    key, found = scores(j)
                    total[h, own, :] += jnp.dot(
                        jnp.exp(found - largest).astype(BF16),
                        values[h, pl.ds(key, KEYS), :],
                        preferred_element_type=F32,
                    )
                    return carry

                lax.fori_loop(0, counts[b], gather, 0)

    for b in range(8):
        own = slice(b * rows, (b + 1) * rows)
        left, right = total[0, own, :], total[1, own, :]
        over = jnp.where(lane < head, left, pltpu.roll(right, head, 1))
        under = jnp.where(lane < head, pltpu.roll(left, head, 1), right)
        out[b] = (over / under).astype(BF16)


def layer(scales, gain, pieces, shard):
    total = 8 * ROWS
    return pl.pallas_call(
        layer_kernel,
        in_specs=[smem()] + [vmem()] * 10,
        out_specs=vmem(),
        out_shape=jax.ShapeDtypeStruct((8, ROWS, 128), BF16),
        scratch_shapes=[
            pltpu.VMEM((8, 4, 32, 384), BF16),
            pltpu.VMEM((2 * ROWS, pieces[0].shape[1]), BF16),
            pltpu.VMEM((8, ROWS), jnp.int32),
            pltpu.VMEM((2, total + ROWS, 128), BF16),
            pltpu.VMEM((2, 128, total), BF16),
            pltpu.VMEM((2, total, 128), BF16),
            pltpu.VMEM((2, total + ROWS, 128), F32),
            pltpu.VMEM((2, ROWS, KEYS), F32),
            pltpu.VMEM((2, ROWS, KEYS), F32),
            pltpu.SMEM((2, 48), jnp.int32),
        ],
        compiler_params=params(),
        name="layer",
    )(scales, gain, *pieces, shard)


def finish_kernel(pieces, *refs):
    shards, (rows, bits, offset, mixed, probs, sums, weights, joined) = refs[:8], refs[8:]
    core, across = lax.axis_index("seq_1"), lax.axis_index("dp_1")
    for i in range(8):
        part = core if i < 4 else 1 - core
        place = lax.rem(across + (0, 2, 1, 3)[i % 4], 4)
        weights[part, :, place] = shards[i][...]
    for source in range(8):
        joined[:, source * 128 : (source + 1) * 128] = pieces[source]
    for part in range(2):
        columns = slice(part * 512, part * 512 + 512)
        moved = jnp.dot(
            joined[...], weights[part].reshape(1024, 512), preferred_element_type=F32
        )
        mixed[:, columns] = (rows[:, columns].astype(F32) + moved).astype(BF16)
    logits = lax.dot_general(
        bits[...], mixed[...], (((1,), (1,)), ((), ())), preferred_element_type=F32
    )
    chance = jax.nn.sigmoid(4.0 * (logits + offset[...]))
    probs[...] = chance
    row = lax.dot_general(
        jnp.ones((8, chance.shape[1]), F32),
        chance,
        (((1,), (1,)), ((), ())),
        preferred_element_type=F32,
        precision=lax.Precision.HIGHEST,
    )
    sums[...] = row[0:1]


def finish(pieces, shards, rows, bits, offset):
    count = rows.shape[0]
    return pl.pallas_call(
        finish_kernel,
        in_specs=[vmem()] * 12,
        out_specs=[vmem()] * 3,
        out_shape=[
            jax.ShapeDtypeStruct(rows.shape, BF16),
            jax.ShapeDtypeStruct((bits.shape[0], count), F32),
            jax.ShapeDtypeStruct((1, bits.shape[0]), F32),
        ],
        scratch_shapes=[
            pltpu.VMEM((2, 8, 4, 32, 512), BF16),
            pltpu.VMEM((count, 1024), BF16),
        ],
        compiler_params=params(),
        name="finish",
    )(pieces, *shards, rows, bits, offset)


def on_device(
    residual_tiles,
    picture_label_tile,
    prenorm_multiplier,
    triple_projector,
    logit_scaling,
    final_projector,
    binarizer_projector,
    binarizer_offset,
):
    rows = residual_tiles[0]
    count, width = rows.shape
    core = lax.axis_index("seq_1")
    member = lax.axis_index(SEQ)
    def from_step(x, k, axis="seq_0"):
        length = lax.axis_size(axis)
        return lax.ppermute(x, axis, [(i, (i - k) % length) for i in range(length)])

    def from_other_core(x):
        return lax.ppermute(x, "seq_1", [(0, 1), (1, 0)])

    marked = jnp.pad(picture_label_tile.astype(BF16), ((0, 15), (0, width - count)))
    load = jnp.concatenate([rows, marked], axis=0)
    near = [load] + [from_step(load, k) for k in (1, 3, 2)]
    pieces = [x for own in near for x in (own, from_other_core(own))]

    owned = jnp.concatenate(
        [
            lax.dynamic_slice_in_dim(triple_projector, member * 128 + 1024 * i, 128, 1)
            for i in range(3)
        ]
        + [lax.dynamic_slice_in_dim(final_projector, core * 512, 512, 1)],
        axis=1,
    )
    owned = copy_for_each(owned, "dp_0")
    shard, mixing = owned[:, :, :384], owned[:, :, 384:]
    shard = copy_for_each(shard, "dp_1")
    mixing, _ = lax.optimization_barrier((mixing, shard))
    mixings = [mixing] + [from_step(mixing, k, "dp_1") for k in (2, 1, 3)]

    pieces, shard = in_vmem((pieces, shard))
    attended = layer(logit_scaling, prenorm_multiplier[None], pieces, shard)
    mixings, attended = lax.optimization_barrier((mixings, attended))
    mixings = in_vmem(mixings)
    mixings = in_vmem(mixings + [from_other_core(m) for m in mixings])
    attended = lax.all_to_all(attended, SEQ, 0, 0, tiled=True)
    mixed, probs, sums = finish(
        in_vmem(attended),
        mixings,
        rows,
        binarizer_projector.T,
        binarizer_offset[:, None],
    )
    sums = jnp.sum(copy_for_each(sums, ("dp_0", "dp_1", "seq_0")), axis=(0, 1))
    marginal = (sums + from_other_core(sums)) / (count * lax.axis_size(ALL))
    code_entropy = -(marginal * jnp.log(marginal) + (1.0 - marginal) * jnp.log(1.0 - marginal))
    bit_codes = (probs - marginal[:, None])[None]
    return (mixed[None], bit_codes, code_entropy)


def solution(mesh):
    finer = Mesh(mesh.devices.reshape(8, 4, 4, 2), ("dp_0", "dp_1", "seq_0", "seq_1"))
    placed = (P(DP, SEQ, None), P(DP, SEQ), P(), P(DP, None), P(), P(DP, None), P(), P())
    return jax.shard_map(
        on_device,
        mesh=finer,
        in_specs=placed,
        out_specs=(P(DP, SEQ, None), P(DP, None, SEQ), P()),
        check_vma=False,
    )
```

```python
import functools
import math

import jax
import jax.numpy as jnp
from jax import lax
from jax.experimental import pallas as pl
from jax.experimental.pallas import tpu as pltpu
from jax.sharding import Mesh
from jax.sharding import PartitionSpec as P

SEQ = ("seq_0", "seq_1")
DP = ("dp_0", "dp_1")
ALL = ("dp_0", "dp_1", "seq_0", "seq_1")

EPS = 1e-06
EXCLUDED = -32768.0
KEYS = 512
ROWS = 256
SAFE = 8.0
LIMIT = 28 * 1024 * 1024
F32 = jnp.float32
BF16 = jnp.bfloat16


def params():
    return pltpu.CompilerParams(vmem_limit_bytes=LIMIT)


def vmem():
    return pl.BlockSpec(memory_space=pltpu.VMEM)


def smem():
    return pl.BlockSpec(memory_space=pltpu.SMEM)


def in_vmem(tree):
    return jax.tree.map(lambda x: pltpu.with_memory_space_constraint(x, pltpu.VMEM), tree)


def copy_for_each(x, axis):
    length = lax.axis_size(axis)
    return lax.all_to_all(jnp.broadcast_to(x[None], (length, *x.shape)), axis, 0, 0, tiled=True)


def layer_kernel(scales, gain, *refs):
    pieces, shards, out = refs[:8], refs[8], refs[9]
    weights, normed, labels, queries, keys, values, total, even, odd, table = refs[10:]
    core, chip = lax.axis_index("seq_1"), lax.axis_index("seq_0")
    first = (2 * chip + core) * 2
    scale = [scales[first] / math.sqrt(64), scales[first + 1] / math.sqrt(64)]
    rows = ROWS
    for i in range(4):
        weights[:, i] = shards[i]
    head = 64
    matrix = weights[...].reshape(normed.shape[1], 384)
    lane = lax.broadcasted_iota(jnp.int32, (rows, 128), 1)
    spot = lax.broadcasted_iota(jnp.int32, (head, rows), 0)
    for pair in range(4):
        step = (0, 1, 3, 2)[pair]
        for side in range(2):
            wide = pieces[2 * pair + side][0:rows].astype(F32)
            inv = lax.rsqrt(jnp.mean(wide * wide, axis=-1, keepdims=True) + EPS)
            normed[side * rows : (side + 1) * rows] = (wide * inv * gain[...]).astype(BF16)
        both = jnp.dot(normed[...], matrix, preferred_element_type=F32).astype(BF16).astype(F32)
        for side in range(2):
            part = core if side == 0 else 1 - core
            block = 2 * lax.rem(chip + step, 4) + part
            start = pl.multiple_of(block * rows, rows)
            joined = both[side * rows : (side + 1) * rows]
            ids = pieces[2 * pair + side][rows : rows + 8, 0:rows].astype(F32)[0:1].astype(jnp.int32)
            labels[pl.ds(block, 1), :] = ids
            same = spot == ids
            bars = jnp.where(same, 0.0, EXCLUDED).astype(F32)
            query = joined[:, 0:128].T
            key = joined[:, 128:256].T
            marks = jnp.where(same, 1.0, 0.0).astype(BF16)
            for h in range(2):
                one = query[h * head : (h + 1) * head]
                inv = lax.rsqrt(jnp.mean(one * one, axis=0, keepdims=True) + EPS)
                queries[h, pl.ds(start, rows), :] = (
                    jnp.concatenate([one * inv * scale[h], bars], axis=0).T.astype(BF16)
                )
                one = key[h * head : (h + 1) * head]
                inv = lax.rsqrt(jnp.mean(one * one, axis=0, keepdims=True) + EPS)
                keys[h, 0:head, pl.ds(start, rows)] = (one * inv).astype(BF16)
                keys[h, head : 2 * head, pl.ds(start, rows)] = marks
            value = joined[:, 256:384]
            values[0, pl.ds(start, rows), :] = jnp.where(lane < head, value, 1.0).astype(BF16)
            values[1, pl.ds(start, rows), :] = jnp.where(
                lane < head, pltpu.roll(value, head, 1), 1.0
            ).astype(BF16)

    every = labels[...]
    opening, closing = every[:, 0:1], every[:, rows - 1 : rows]
    below = jnp.zeros((8, rows), jnp.int32)
    upto = jnp.zeros((8, rows), jnp.int32)
    for b in range(8):
        below += (every[b : b + 1] < opening).astype(jnp.int32)
        upto += (every[b : b + 1] <= closing).astype(jnp.int32)
    low = jnp.sum(below, axis=1, keepdims=True)
    high = jnp.sum(upto, axis=1, keepdims=True)
    low = low & -128
    counts = lax.shift_right_logical(high - low + (KEYS - 1), 9)
    low = jnp.minimum(low, 2048 - counts * KEYS)
    lows = [low[b, 0] for b in range(8)]
    counts = [counts[b, 0] for b in range(8)]
    total[...] = jnp.zeros(total.shape, F32)

    pairs = jnp.int32(0)
    for b in range(8):

        def note(s, pairs, b=b):
            table[0, pairs] = jnp.int32(b * rows)
            table[1, pairs] = lows[b] + s * KEYS
            return pairs + 1

        pairs = lax.fori_loop(0, counts[b], note, pairs)
    for spare in range(2):
        table[0, pairs + spare] = jnp.int32(8 * rows)
        table[1, pairs + spare] = jnp.int32(0)

    def score(j, into):
        row = pl.multiple_of(table[0, j], rows)
        key = pl.multiple_of(table[1, j], 128)
        for h in range(2):
            into[h] = jnp.dot(
                queries[h, pl.ds(row, rows), :],
                keys[h, :, pl.ds(key, KEYS)],
                preferred_element_type=F32,
            )

    def absorb(j, source):
        row = pl.multiple_of(table[0, j], rows)
        key = pl.multiple_of(table[1, j], 128)
        for h in range(2):
            total[h, pl.ds(row, rows), :] += jnp.dot(
                jnp.exp(source[h]).astype(BF16),
                values[h, pl.ds(key, KEYS), :],
                preferred_element_type=F32,
            )

    small = jnp.maximum(scales[first], scales[first + 1]) <= SAFE

    @pl.when(small)
    def _():
        score(0, even)

        def twice(j, carry):
            score(2 * j + 1, odd)
            absorb(2 * j, even)
            score(2 * j + 2, even)
            absorb(2 * j + 1, odd)
            return carry

        lax.fori_loop(0, (pairs + 1) // 2, twice, 0)

    @pl.when(jnp.logical_not(small))
    def _():
        for b in range(8):
            own = pl.ds(b * rows, rows)
            for h in range(2):

                def scores(j, b=b, h=h, own=own):
                    key = pl.multiple_of(lows[b] + j * KEYS, 128)
                    return key, jnp.dot(
                        queries[h, own, :], keys[h, :, pl.ds(key, KEYS)], preferred_element_type=F32
                    )

                def top(j, most, scores=scores):
                    return jnp.maximum(most, jnp.max(scores(j)[1], axis=-1, keepdims=True))

                largest = lax.fori_loop(
                    0, counts[b], top, jnp.full((rows, 1), 2.0 * EXCLUDED, F32)
                )

                def gather(j, carry, h=h, own=own, scores=scores, largest=largest):
                    key, found = scores(j)
                    total[h, own, :] += jnp.dot(
                        jnp.exp(found - largest).astype(BF16),
                        values[h, pl.ds(key, KEYS), :],
                        preferred_element_type=F32,
                    )
                    return carry

                lax.fori_loop(0, counts[b], gather, 0)

    for b in range(8):
        own = slice(b * rows, (b + 1) * rows)
        left, right = total[0, own, :], total[1, own, :]
        over = jnp.where(lane < head, left, pltpu.roll(right, head, 1))
        under = jnp.where(lane < head, pltpu.roll(left, head, 1), right)
        out[b] = (over / under).astype(BF16)


def layer(scales, gain, pieces, shard):
    total = 8 * ROWS
    return pl.pallas_call(
        layer_kernel,
        in_specs=[smem()] + [vmem()] * 10,
        out_specs=vmem(),
        out_shape=jax.ShapeDtypeStruct((8, ROWS, 128), BF16),
        scratch_shapes=[
            pltpu.VMEM((8, 4, 32, 384), BF16),
            pltpu.VMEM((2 * ROWS, pieces[0].shape[1]), BF16),
            pltpu.VMEM((8, ROWS), jnp.int32),
            pltpu.VMEM((2, total + ROWS, 128), BF16),
            pltpu.VMEM((2, 128, total), BF16),
            pltpu.VMEM((2, total, 128), BF16),
            pltpu.VMEM((2, total + ROWS, 128), F32),
            pltpu.VMEM((2, ROWS, KEYS), F32),
            pltpu.VMEM((2, ROWS, KEYS), F32),
            pltpu.SMEM((2, 48), jnp.int32),
        ],
        compiler_params=params(),
        name="layer",
    )(scales, gain, *pieces, shard)


def finish_kernel(pieces, *refs):
    shards, (rows, bits, offset, mixed, probs, sums, weights, joined, sems) = refs[:8], refs[8:]
    core, across = lax.axis_index("seq_1"), lax.axis_index("dp_1")
    copies = []
    for i in range(4):
        place = lax.rem(across + (0, 2, 1, 3)[i], 4)
        copies.append(
            pltpu.make_async_copy(shards[i], weights.at[core, :, place], sems.at[i])
        )
        copies[i].start()
    for i in range(4):
        place = lax.rem(across + (0, 2, 1, 3)[i], 4)
        weights[1 - core, :, place] = shards[4 + i][...]
    for source in range(8):
        joined[:, source * 128 : (source + 1) * 128] = pieces[source]
    for turn, part in ((0, 1 - core), (1, core)):
        if turn:
            for copy in copies:
                copy.wait()
        columns = pl.ds(pl.multiple_of(part * 512, 512), 512)
        moved = jnp.dot(
            joined[...], weights[part].reshape(1024, 512), preferred_element_type=F32
        )
        mixed[:, columns] = (rows[:, columns].astype(F32) + moved).astype(BF16)
    logits = lax.dot_general(
        bits[...], mixed[...], (((1,), (1,)), ((), ())), preferred_element_type=F32
    )
    chance = jax.nn.sigmoid(4.0 * (logits + offset[...]))
    probs[...] = chance
    row = lax.dot_general(
        jnp.ones((8, chance.shape[1]), F32),
        chance,
        (((1,), (1,)), ((), ())),
        preferred_element_type=F32,
        precision=lax.Precision.HIGHEST,
    )
    sums[...] = row[0:1]


def finish(pieces, shards, rows, bits, offset):
    count = rows.shape[0]
    return pl.pallas_call(
        finish_kernel,
        in_specs=[vmem()] + [pl.BlockSpec(memory_space=pl.ANY)] * 4 + [vmem()] * 7,
        out_specs=[vmem()] * 3,
        out_shape=[
            jax.ShapeDtypeStruct(rows.shape, BF16),
            jax.ShapeDtypeStruct((bits.shape[0], count), F32),
            jax.ShapeDtypeStruct((1, bits.shape[0]), F32),
        ],
        scratch_shapes=[
            pltpu.VMEM((2, 8, 4, 32, 512), BF16),
            pltpu.VMEM((count, 1024), BF16),
            pltpu.SemaphoreType.DMA((4,)),
        ],
        compiler_params=params(),
        name="finish",
    )(pieces, *shards, rows, bits, offset)


def on_device(
    residual_tiles,
    picture_label_tile,
    prenorm_multiplier,
    triple_projector,
    logit_scaling,
    final_projector,
    binarizer_projector,
    binarizer_offset,
):
    rows = residual_tiles[0]
    count, width = rows.shape
    core = lax.axis_index("seq_1")
    member = lax.axis_index(SEQ)
    def from_step(x, k, axis="seq_0"):
        length = lax.axis_size(axis)
        return lax.ppermute(x, axis, [(i, (i - k) % length) for i in range(length)])

    def from_other_core(x):
        return lax.ppermute(x, "seq_1", [(0, 1), (1, 0)])

    marked = jnp.pad(picture_label_tile.astype(BF16), ((0, 15), (0, width - count)))
    load = jnp.concatenate([rows, marked], axis=0)
    near = [load] + [from_step(load, k) for k in (1, 3, 2)]

    owned = jnp.concatenate(
        [
            lax.dynamic_slice_in_dim(triple_projector, member * 128 + 1024 * i, 128, 1)
            for i in range(3)
        ]
        + [lax.dynamic_slice_in_dim(final_projector, core * 512, 512, 1)],
        axis=1,
    )
    owned = copy_for_each(owned, "dp_0")
    shard, mixing = owned[:, :, :384], owned[:, :, 384:]
    shard = copy_for_each(shard, "dp_1")
    near[1], mixing = lax.optimization_barrier((near[1], mixing))
    pieces = [x for own in near for x in (own, from_other_core(own))]
    mixing, _ = lax.optimization_barrier((mixing, shard))
    mixings = [mixing] + [from_step(mixing, k, "dp_1") for k in (2, 1, 3)]

    pieces, shard = in_vmem((pieces, shard))
    attended = layer(logit_scaling, prenorm_multiplier[None], pieces, shard)
    mixings, attended = lax.optimization_barrier((mixings, attended))
    mixings = [pltpu.with_memory_space_constraint(m, pltpu.HBM) for m in mixings]
    mixings = mixings + in_vmem([from_other_core(m) for m in mixings])
    attended = lax.all_to_all(attended, SEQ, 0, 0, tiled=True)
    mixed, probs, sums = finish(
        in_vmem(attended),
        mixings,
        rows,
        binarizer_projector.T,
        binarizer_offset[:, None],
    )
    sums = jnp.sum(copy_for_each(sums, ("dp_0", "dp_1", "seq_0")), axis=(0, 1))
    marginal = (sums + from_other_core(sums)) / (count * lax.axis_size(ALL))
    code_entropy = -(marginal * jnp.log(marginal) + (1.0 - marginal) * jnp.log(1.0 - marginal))
    bit_codes = (probs - marginal[:, None])[None]
    return (mixed[None], bit_codes, code_entropy)


def solution(mesh):
    finer = Mesh(mesh.devices.reshape(8, 4, 4, 2), ("dp_0", "dp_1", "seq_0", "seq_1"))
    placed = (P(DP, SEQ, None), P(DP, SEQ), P(), P(DP, None), P(), P(DP, None), P(), P())
    return jax.shard_map(
        on_device,
        mesh=finer,
        in_specs=placed,
        out_specs=(P(DP, SEQ, None), P(DP, None, SEQ), P()),
        check_vma=False,
    )
```

```python
import functools
import math

import jax
import jax.numpy as jnp
from jax import lax
from jax.experimental import pallas as pl
from jax.experimental.pallas import tpu as pltpu
from jax.sharding import Mesh
from jax.sharding import PartitionSpec as P

SEQ = ("seq_0", "seq_1")
DP = ("dp_0", "dp_1")
ALL = ("dp_0", "dp_1", "seq_0", "seq_1")

EPS = 1e-06
EXCLUDED = -32768.0
KEYS = 512
ROWS = 256
SAFE = 8.0
LIMIT = 28 * 1024 * 1024
F32 = jnp.float32
BF16 = jnp.bfloat16


def params():
    return pltpu.CompilerParams(vmem_limit_bytes=LIMIT)


def vmem():
    return pl.BlockSpec(memory_space=pltpu.VMEM)


def smem():
    return pl.BlockSpec(memory_space=pltpu.SMEM)


def in_vmem(tree):
    return jax.tree.map(lambda x: pltpu.with_memory_space_constraint(x, pltpu.VMEM), tree)


def copy_for_each(x, axis):
    length = lax.axis_size(axis)
    return lax.all_to_all(jnp.broadcast_to(x[None], (length, *x.shape)), axis, 0, 0, tiled=True)


def pack_kernel(triple, final, out, held, sems):
    chip, core = lax.axis_index("seq_0"), lax.axis_index("seq_1")
    member = 2 * chip + core
    copies = [
        pltpu.make_async_copy(
            triple.at[:, pl.ds(pl.multiple_of(1024 * i + member * 128, 128), 128)],
            held.at[:, pl.ds(128 * i, 128)],
            sems.at[i],
        )
        for i in range(3)
    ]
    copies.append(
        pltpu.make_async_copy(
            final.at[:, pl.ds(pl.multiple_of(core * 512, 512), 512)],
            held.at[:, pl.ds(384, 512)],
            sems.at[3],
        )
    )
    for copy in copies:
        copy.start()
    for copy in copies:
        copy.wait()
    for i in range(out.shape[0]):
        out[i] = held[...]


def pack(triple, final, length):
    shard = triple.shape[0]
    anywhere = pl.BlockSpec(memory_space=pltpu.HBM)
    return pl.pallas_call(
        pack_kernel,
        in_specs=[anywhere, anywhere],
        out_specs=vmem(),
        out_shape=jax.ShapeDtypeStruct((length, shard, 896), BF16),
        scratch_shapes=[pltpu.VMEM((shard, 896), BF16), pltpu.SemaphoreType.DMA((4,))],
        compiler_params=params(),
        name="pack",
    )(triple, final)


def layer_kernel(scales, gain, *refs):
    pieces, shards, out = refs[:8], refs[8], refs[9]
    weights, normed, labels, queries, keys, values, total, even, odd, table = refs[10:]
    core, chip = lax.axis_index("seq_1"), lax.axis_index("seq_0")
    first = (2 * chip + core) * 2
    scale = [scales[first] / math.sqrt(64), scales[first + 1] / math.sqrt(64)]
    rows = ROWS
    for i in range(4):
        weights[:, i] = shards[i]
    head = 64
    matrix = weights[...].reshape(normed.shape[1], 384)
    lane = lax.broadcasted_iota(jnp.int32, (rows, 128), 1)
    spot = lax.broadcasted_iota(jnp.int32, (head, rows), 0)
    for pair in range(4):
        step = (0, 1, 3, 2)[pair]
        for side in range(2):
            wide = pieces[2 * pair + side][0:rows].astype(F32)
            inv = lax.rsqrt(jnp.mean(wide * wide, axis=-1, keepdims=True) + EPS)
            normed[side * rows : (side + 1) * rows] = (wide * inv * gain[...]).astype(BF16)
        both = jnp.dot(normed[...], matrix, preferred_element_type=F32).astype(BF16).astype(F32)
        for side in range(2):
            part = core if side == 0 else 1 - core
            block = 2 * lax.rem(chip + step, 4) + part
            start = pl.multiple_of(block * rows, rows)
            joined = both[side * rows : (side + 1) * rows]
            ids = pieces[2 * pair + side][rows : rows + 8, 0:rows].astype(F32)[0:1].astype(jnp.int32)
            labels[pl.ds(block, 1), :] = ids
            same = spot == ids
            bars = jnp.where(same, 0.0, EXCLUDED).astype(F32)
            query = joined[:, 0:128].T
            key = joined[:, 128:256].T
            marks = jnp.where(same, 1.0, 0.0).astype(BF16)
            for h in range(2):
                one = query[h * head : (h + 1) * head]
                inv = lax.rsqrt(jnp.mean(one * one, axis=0, keepdims=True) + EPS)
                queries[h, pl.ds(start, rows), :] = (
                    jnp.concatenate([one * inv * scale[h], bars], axis=0).T.astype(BF16)
                )
                one = key[h * head : (h + 1) * head]
                inv = lax.rsqrt(jnp.mean(one * one, axis=0, keepdims=True) + EPS)
                keys[h, 0:head, pl.ds(start, rows)] = (one * inv).astype(BF16)
                keys[h, head : 2 * head, pl.ds(start, rows)] = marks
            value = joined[:, 256:384]
            values[0, pl.ds(start, rows), :] = jnp.where(lane < head, value, 1.0).astype(BF16)
            values[1, pl.ds(start, rows), :] = jnp.where(
                lane < head, pltpu.roll(value, head, 1), 1.0
            ).astype(BF16)

    every = labels[...]
    opening, closing = every[:, 0:1], every[:, rows - 1 : rows]
    below = jnp.zeros((8, rows), jnp.int32)
    upto = jnp.zeros((8, rows), jnp.int32)
    for b in range(8):
        below += (every[b : b + 1] < opening).astype(jnp.int32)
        upto += (every[b : b + 1] <= closing).astype(jnp.int32)
    low = jnp.sum(below, axis=1, keepdims=True)
    high = jnp.sum(upto, axis=1, keepdims=True)
    low = low & -128
    counts = lax.shift_right_logical(high - low + (KEYS - 1), 9)
    low = jnp.minimum(low, 2048 - counts * KEYS)
    lows = [low[b, 0] for b in range(8)]
    counts = [counts[b, 0] for b in range(8)]
    total[...] = jnp.zeros(total.shape, F32)

    pairs = jnp.int32(0)
    for b in range(8):

        def note(s, pairs, b=b):
            table[0, pairs] = jnp.int32(b * rows)
            table[1, pairs] = lows[b] + s * KEYS
            return pairs + 1

        pairs = lax.fori_loop(0, counts[b], note, pairs)
    for spare in range(2):
        table[0, pairs + spare] = jnp.int32(8 * rows)
        table[1, pairs + spare] = jnp.int32(0)

    def score(j, into):
        row = pl.multiple_of(table[0, j], rows)
        key = pl.multiple_of(table[1, j], 128)
        for h in range(2):
            into[h] = jnp.dot(
                queries[h, pl.ds(row, rows), :],
                keys[h, :, pl.ds(key, KEYS)],
                preferred_element_type=F32,
            )

    def absorb(j, source):
        row = pl.multiple_of(table[0, j], rows)
        key = pl.multiple_of(table[1, j], 128)
        for h in range(2):
            total[h, pl.ds(row, rows), :] += jnp.dot(
                jnp.exp(source[h]).astype(BF16),
                values[h, pl.ds(key, KEYS), :],
                preferred_element_type=F32,
            )

    small = jnp.maximum(scales[first], scales[first + 1]) <= SAFE

    @pl.when(small)
    def _():
        score(0, even)

        def twice(j, carry):
            score(2 * j + 1, odd)
            absorb(2 * j, even)
            score(2 * j + 2, even)
            absorb(2 * j + 1, odd)
            return carry

        lax.fori_loop(0, (pairs + 1) // 2, twice, 0)

    @pl.when(jnp.logical_not(small))
    def _():
        for b in range(8):
            own = pl.ds(b * rows, rows)
            for h in range(2):

                def scores(j, b=b, h=h, own=own):
                    key = pl.multiple_of(lows[b] + j * KEYS, 128)
                    return key, jnp.dot(
                        queries[h, own, :], keys[h, :, pl.ds(key, KEYS)], preferred_element_type=F32
                    )

                def top(j, most, scores=scores):
                    return jnp.maximum(most, jnp.max(scores(j)[1], axis=-1, keepdims=True))

                largest = lax.fori_loop(
                    0, counts[b], top, jnp.full((rows, 1), 2.0 * EXCLUDED, F32)
                )

                def gather(j, carry, h=h, own=own, scores=scores, largest=largest):
                    key, found = scores(j)
                    total[h, own, :] += jnp.dot(
                        jnp.exp(found - largest).astype(BF16),
                        values[h, pl.ds(key, KEYS), :],
                        preferred_element_type=F32,
                    )
                    return carry

                lax.fori_loop(0, counts[b], gather, 0)

    for b in range(8):
        own = slice(b * rows, (b + 1) * rows)
        left, right = total[0, own, :], total[1, own, :]
        over = jnp.where(lane < head, left, pltpu.roll(right, head, 1))
        under = jnp.where(lane < head, pltpu.roll(left, head, 1), right)
        out[b] = (over / under).astype(BF16)


def layer(scales, gain, pieces, shard):
    total = 8 * ROWS
    return pl.pallas_call(
        layer_kernel,
        in_specs=[smem()] + [vmem()] * 10,
        out_specs=vmem(),
        out_shape=jax.ShapeDtypeStruct((8, ROWS, 128), BF16),
        scratch_shapes=[
            pltpu.VMEM((8, 4, 32, 384), BF16),
            pltpu.VMEM((2 * ROWS, pieces[0].shape[1]), BF16),
            pltpu.VMEM((8, ROWS), jnp.int32),
            pltpu.VMEM((2, total + ROWS, 128), BF16),
            pltpu.VMEM((2, 128, total), BF16),
            pltpu.VMEM((2, total, 128), BF16),
            pltpu.VMEM((2, total + ROWS, 128), F32),
            pltpu.VMEM((2, ROWS, KEYS), F32),
            pltpu.VMEM((2, ROWS, KEYS), F32),
            pltpu.SMEM((2, 48), jnp.int32),
        ],
        compiler_params=params(),
        name="layer",
    )(scales, gain, *pieces, shard)


def finish_kernel(pieces, *refs):
    shards, (rows, bits, offset, mixed, probs, sums, weights, joined, sems) = refs[:8], refs[8:]
    core, across = lax.axis_index("seq_1"), lax.axis_index("dp_1")
    copies = []
    for i in range(4):
        place = lax.rem(across + (0, 2, 1, 3)[i], 4)
        copies.append(
            pltpu.make_async_copy(shards[i], weights.at[core, :, place], sems.at[i])
        )
        copies[i].start()
    for i in range(4):
        place = lax.rem(across + (0, 2, 1, 3)[i], 4)
        weights[1 - core, :, place] = shards[4 + i][...]
    for source in range(8):
        joined[:, source * 128 : (source + 1) * 128] = pieces[source]
    for turn, part in ((0, 1 - core), (1, core)):
        if turn:
            for copy in copies:
                copy.wait()
        columns = pl.ds(pl.multiple_of(part * 512, 512), 512)
        moved = jnp.dot(
            joined[...], weights[part].reshape(1024, 512), preferred_element_type=F32
        )
        mixed[:, columns] = (rows[:, columns].astype(F32) + moved).astype(BF16)
    logits = lax.dot_general(
        bits[...], mixed[...], (((1,), (1,)), ((), ())), preferred_element_type=F32
    )
    chance = jax.nn.sigmoid(4.0 * (logits + offset[...]))
    probs[...] = chance
    row = lax.dot_general(
        jnp.ones((8, chance.shape[1]), F32),
        chance,
        (((1,), (1,)), ((), ())),
        preferred_element_type=F32,
        precision=lax.Precision.HIGHEST,
    )
    sums[...] = row[0:1]


def finish(pieces, shards, rows, bits, offset):
    count = rows.shape[0]
    return pl.pallas_call(
        finish_kernel,
        in_specs=[vmem()] + [pl.BlockSpec(memory_space=pl.ANY)] * 4 + [vmem()] * 7,
        out_specs=[vmem()] * 3,
        out_shape=[
            jax.ShapeDtypeStruct(rows.shape, BF16),
            jax.ShapeDtypeStruct((bits.shape[0], count), F32),
            jax.ShapeDtypeStruct((1, bits.shape[0]), F32),
        ],
        scratch_shapes=[
            pltpu.VMEM((2, 8, 4, 32, 512), BF16),
            pltpu.VMEM((count, 1024), BF16),
            pltpu.SemaphoreType.DMA((4,)),
        ],
        compiler_params=params(),
        name="finish",
    )(pieces, *shards, rows, bits, offset)


def on_device(
    residual_tiles,
    picture_label_tile,
    prenorm_multiplier,
    triple_projector,
    logit_scaling,
    final_projector,
    binarizer_projector,
    binarizer_offset,
):
    rows = residual_tiles[0]
    count, width = rows.shape
    core = lax.axis_index("seq_1")
    member = lax.axis_index(SEQ)
    def from_step(x, k, axis="seq_0"):
        length = lax.axis_size(axis)
        return lax.ppermute(x, axis, [(i, (i - k) % length) for i in range(length)])

    def from_other_core(x):
        return lax.ppermute(x, "seq_1", [(0, 1), (1, 0)])

    marked = jnp.pad(picture_label_tile.astype(BF16), ((0, 15), (0, width - count)))
    load = jnp.concatenate([rows, marked], axis=0)
    near = [load] + [from_step(load, k) for k in (1, 3, 2)]

    in_hbm = lambda x: pltpu.with_memory_space_constraint(x, pltpu.HBM)
    owned = pack(in_hbm(triple_projector), in_hbm(final_projector), lax.axis_size("dp_0"))
    owned = lax.all_to_all(owned, "dp_0", 0, 0, tiled=True)
    shard, mixing = owned[:, :, :384], owned[:, :, 384:]
    shard, mixing = lax.optimization_barrier((shard, mixing))
    shard = copy_for_each(shard, "dp_1")
    pieces = [x for own in near for x in (own, from_other_core(own))]
    mixing, _ = lax.optimization_barrier((mixing, shard))
    mixings = [mixing] + [from_step(mixing, k, "dp_1") for k in (2, 1, 3)]

    pieces, shard = in_vmem((pieces, shard))
    attended = layer(logit_scaling, prenorm_multiplier[None], pieces, shard)
    mixings, attended = lax.optimization_barrier((mixings, attended))
    mixings = [in_hbm(m) for m in mixings]
    mixings = mixings + in_vmem([from_other_core(m) for m in mixings])
    attended = lax.all_to_all(attended, SEQ, 0, 0, tiled=True)
    mixed, probs, sums = finish(
        in_vmem(attended),
        mixings,
        rows,
        binarizer_projector.T,
        binarizer_offset[:, None],
    )
    sums = jnp.sum(copy_for_each(sums, ("dp_0", "dp_1", "seq_0")), axis=(0, 1))
    marginal = (sums + from_other_core(sums)) / (count * lax.axis_size(ALL))
    code_entropy = -(marginal * jnp.log(marginal) + (1.0 - marginal) * jnp.log(1.0 - marginal))
    bit_codes = (probs - marginal[:, None])[None]
    return (mixed[None], bit_codes, code_entropy)


def solution(mesh):
    finer = Mesh(mesh.devices.reshape(8, 4, 4, 2), ("dp_0", "dp_1", "seq_0", "seq_1"))
    placed = (P(DP, SEQ, None), P(DP, SEQ), P(), P(DP, None), P(), P(DP, None), P(), P())
    return jax.shard_map(
        on_device,
        mesh=finer,
        in_specs=placed,
        out_specs=(P(DP, SEQ, None), P(DP, None, SEQ), P()),
        check_vma=False,
    )
```

```python
import functools
import math

import jax
import jax.numpy as jnp
from jax import lax
from jax.experimental import pallas as pl
from jax.experimental.pallas import tpu as pltpu
from jax.sharding import Mesh
from jax.sharding import PartitionSpec as P

SEQ = ("seq_0", "seq_1")
DP = ("dp_0", "dp_1")
ALL = ("dp_0", "dp_1", "seq_0", "seq_1")

EPS = 1e-06
EXCLUDED = -32768.0
KEYS = 512
ROWS = 256
SAFE = 8.0
LIMIT = 28 * 1024 * 1024
F32 = jnp.float32
BF16 = jnp.bfloat16


def params():
    return pltpu.CompilerParams(vmem_limit_bytes=LIMIT)


def vmem():
    return pl.BlockSpec(memory_space=pltpu.VMEM)


def smem():
    return pl.BlockSpec(memory_space=pltpu.SMEM)


def in_vmem(tree):
    return jax.tree.map(lambda x: pltpu.with_memory_space_constraint(x, pltpu.VMEM), tree)


def copy_for_each(x, axis):
    length = lax.axis_size(axis)
    return lax.all_to_all(jnp.broadcast_to(x[None], (length, *x.shape)), axis, 0, 0, tiled=True)


def pack_kernel(triple, final, out, held, sems):
    chip, core = lax.axis_index("seq_0"), lax.axis_index("seq_1")
    member = 2 * chip + core
    copies = [
        pltpu.make_async_copy(
            triple.at[:, pl.ds(pl.multiple_of(1024 * i + member * 128, 128), 128)],
            held.at[:, pl.ds(128 * i, 128)],
            sems.at[i],
        )
        for i in range(3)
    ]
    copies.append(
        pltpu.make_async_copy(
            final.at[:, pl.ds(pl.multiple_of(core * 512, 512), 512)],
            held.at[:, pl.ds(384, 512)],
            sems.at[3],
        )
    )
    for copy in copies:
        copy.start()
    for copy in copies:
        copy.wait()
    for i in range(out.shape[0]):
        out[i] = held[...]


def pack(triple, final, length):
    shard = triple.shape[0]
    anywhere = pl.BlockSpec(memory_space=pltpu.HBM)
    return pl.pallas_call(
        pack_kernel,
        in_specs=[anywhere, anywhere],
        out_specs=vmem(),
        out_shape=jax.ShapeDtypeStruct((length, shard, 896), BF16),
        scratch_shapes=[pltpu.VMEM((shard, 896), BF16), pltpu.SemaphoreType.DMA((4,))],
        compiler_params=params(),
        name="pack",
    )(triple, final)


def spread_kernel(both, shard, mixing):
    for i in range(shard.shape[0]):
        shard[i] = both[:, :, 0:384]
    mixing[...] = both[:, :, 384:896]


def spread(both, length):
    lead = both.shape[:2]
    return pl.pallas_call(
        spread_kernel,
        in_specs=[vmem()],
        out_specs=[vmem()] * 2,
        out_shape=[
            jax.ShapeDtypeStruct((length, *lead, 384), BF16),
            jax.ShapeDtypeStruct((*lead, 512), BF16),
        ],
        compiler_params=params(),
        name="spread",
    )(both)


def layer_kernel(scales, gain, *refs):
    pieces, shards, out = refs[:8], refs[8], refs[9]
    weights, normed, labels, queries, keys, values, total, even, odd, table = refs[10:]
    core, chip = lax.axis_index("seq_1"), lax.axis_index("seq_0")
    first = (2 * chip + core) * 2
    scale = [scales[first] / math.sqrt(64), scales[first + 1] / math.sqrt(64)]
    rows = ROWS
    for i in range(4):
        weights[:, i] = shards[i]
    head = 64
    matrix = weights[...].reshape(normed.shape[1], 384)
    lane = lax.broadcasted_iota(jnp.int32, (rows, 128), 1)
    spot = lax.broadcasted_iota(jnp.int32, (head, rows), 0)
    for pair in range(4):
        step = (0, 1, 3, 2)[pair]
        for side in range(2):
            wide = pieces[2 * pair + side][0:rows].astype(F32)
            inv = lax.rsqrt(jnp.mean(wide * wide, axis=-1, keepdims=True) + EPS)
            normed[side * rows : (side + 1) * rows] = (wide * inv * gain[...]).astype(BF16)
        both = jnp.dot(normed[...], matrix, preferred_element_type=F32).astype(BF16).astype(F32)
        for side in range(2):
            part = core if side == 0 else 1 - core
            block = 2 * lax.rem(chip + step, 4) + part
            start = pl.multiple_of(block * rows, rows)
            joined = both[side * rows : (side + 1) * rows]
            ids = pieces[2 * pair + side][rows : rows + 8, 0:rows].astype(F32)[0:1].astype(jnp.int32)
            labels[pl.ds(block, 1), :] = ids
            same = spot == ids
            bars = jnp.where(same, 0.0, EXCLUDED).astype(F32)
            query = joined[:, 0:128].T
            key = joined[:, 128:256].T
            marks = jnp.where(same, 1.0, 0.0).astype(BF16)
            for h in range(2):
                one = query[h * head : (h + 1) * head]
                inv = lax.rsqrt(jnp.mean(one * one, axis=0, keepdims=True) + EPS)
                queries[h, pl.ds(start, rows), :] = (
                    jnp.concatenate([one * inv * scale[h], bars], axis=0).T.astype(BF16)
                )
                one = key[h * head : (h + 1) * head]
                inv = lax.rsqrt(jnp.mean(one * one, axis=0, keepdims=True) + EPS)
                keys[h, 0:head, pl.ds(start, rows)] = (one * inv).astype(BF16)
                keys[h, head : 2 * head, pl.ds(start, rows)] = marks
            value = joined[:, 256:384]
            values[0, pl.ds(start, rows), :] = jnp.where(lane < head, value, 1.0).astype(BF16)
            values[1, pl.ds(start, rows), :] = jnp.where(
                lane < head, pltpu.roll(value, head, 1), 1.0
            ).astype(BF16)

    every = labels[...]
    opening, closing = every[:, 0:1], every[:, rows - 1 : rows]
    below = jnp.zeros((8, rows), jnp.int32)
    upto = jnp.zeros((8, rows), jnp.int32)
    for b in range(8):
        below += (every[b : b + 1] < opening).astype(jnp.int32)
        upto += (every[b : b + 1] <= closing).astype(jnp.int32)
    low = jnp.sum(below, axis=1, keepdims=True)
    high = jnp.sum(upto, axis=1, keepdims=True)
    low = low & -128
    counts = lax.shift_right_logical(high - low + (KEYS - 1), 9)
    low = jnp.minimum(low, 2048 - counts * KEYS)
    lows = [low[b, 0] for b in range(8)]
    counts = [counts[b, 0] for b in range(8)]
    total[...] = jnp.zeros(total.shape, F32)

    pairs = jnp.int32(0)
    for b in range(8):

        def note(s, pairs, b=b):
            table[0, pairs] = jnp.int32(b * rows)
            table[1, pairs] = lows[b] + s * KEYS
            return pairs + 1

        pairs = lax.fori_loop(0, counts[b], note, pairs)
    for spare in range(2):
        table[0, pairs + spare] = jnp.int32(8 * rows)
        table[1, pairs + spare] = jnp.int32(0)

    def score(j, into):
        row = pl.multiple_of(table[0, j], rows)
        key = pl.multiple_of(table[1, j], 128)
        for h in range(2):
            into[h] = jnp.dot(
                queries[h, pl.ds(row, rows), :],
                keys[h, :, pl.ds(key, KEYS)],
                preferred_element_type=F32,
            )

    def absorb(j, source):
        row = pl.multiple_of(table[0, j], rows)
        key = pl.multiple_of(table[1, j], 128)
        for h in range(2):
            total[h, pl.ds(row, rows), :] += jnp.dot(
                jnp.exp(source[h]).astype(BF16),
                values[h, pl.ds(key, KEYS), :],
                preferred_element_type=F32,
            )

    small = jnp.maximum(scales[first], scales[first + 1]) <= SAFE

    @pl.when(small)
    def _():
        score(0, even)

        def twice(j, carry):
            score(2 * j + 1, odd)
            absorb(2 * j, even)
            score(2 * j + 2, even)
            absorb(2 * j + 1, odd)
            return carry

        lax.fori_loop(0, (pairs + 1) // 2, twice, 0)

    @pl.when(jnp.logical_not(small))
    def _():
        for b in range(8):
            own = pl.ds(b * rows, rows)
            for h in range(2):

                def scores(j, b=b, h=h, own=own):
                    key = pl.multiple_of(lows[b] + j * KEYS, 128)
                    return key, jnp.dot(
                        queries[h, own, :], keys[h, :, pl.ds(key, KEYS)], preferred_element_type=F32
                    )

                def top(j, most, scores=scores):
                    return jnp.maximum(most, jnp.max(scores(j)[1], axis=-1, keepdims=True))

                largest = lax.fori_loop(
                    0, counts[b], top, jnp.full((rows, 1), 2.0 * EXCLUDED, F32)
                )

                def gather(j, carry, h=h, own=own, scores=scores, largest=largest):
                    key, found = scores(j)
                    total[h, own, :] += jnp.dot(
                        jnp.exp(found - largest).astype(BF16),
                        values[h, pl.ds(key, KEYS), :],
                        preferred_element_type=F32,
                    )
                    return carry

                lax.fori_loop(0, counts[b], gather, 0)

    for b in range(8):
        own = slice(b * rows, (b + 1) * rows)
        left, right = total[0, own, :], total[1, own, :]
        over = jnp.where(lane < head, left, pltpu.roll(right, head, 1))
        under = jnp.where(lane < head, pltpu.roll(left, head, 1), right)
        out[b] = (over / under).astype(BF16)


def layer(scales, gain, pieces, shard):
    total = 8 * ROWS
    return pl.pallas_call(
        layer_kernel,
        in_specs=[smem()] + [vmem()] * 10,
        out_specs=vmem(),
        out_shape=jax.ShapeDtypeStruct((8, ROWS, 128), BF16),
        scratch_shapes=[
            pltpu.VMEM((8, 4, 32, 384), BF16),
            pltpu.VMEM((2 * ROWS, pieces[0].shape[1]), BF16),
            pltpu.VMEM((8, ROWS), jnp.int32),
            pltpu.VMEM((2, total + ROWS, 128), BF16),
            pltpu.VMEM((2, 128, total), BF16),
            pltpu.VMEM((2, total, 128), BF16),
            pltpu.VMEM((2, total + ROWS, 128), F32),
            pltpu.VMEM((2, ROWS, KEYS), F32),
            pltpu.VMEM((2, ROWS, KEYS), F32),
            pltpu.SMEM((2, 48), jnp.int32),
        ],
        compiler_params=params(),
        name="layer",
    )(scales, gain, *pieces, shard)


def finish_kernel(pieces, *refs):
    shards, (rows, bits, offset, mixed, probs, sums, weights, joined, sems) = refs[:8], refs[8:]
    core, across = lax.axis_index("seq_1"), lax.axis_index("dp_1")
    copies = []
    for i in range(4):
        place = lax.rem(across + (0, 2, 1, 3)[i], 4)
        copies.append(
            pltpu.make_async_copy(shards[i], weights.at[core, :, place], sems.at[i])
        )
        copies[i].start()
    for i in range(4):
        place = lax.rem(across + (0, 2, 1, 3)[i], 4)
        weights[1 - core, :, place] = shards[4 + i][...]
    for source in range(8):
        joined[:, source * 128 : (source + 1) * 128] = pieces[source]
    for turn, part in ((0, 1 - core), (1, core)):
        if turn:
            for copy in copies:
                copy.wait()
        columns = pl.ds(pl.multiple_of(part * 512, 512), 512)
        moved = jnp.dot(
            joined[...], weights[part].reshape(1024, 512), preferred_element_type=F32
        )
        mixed[:, columns] = (rows[:, columns].astype(F32) + moved).astype(BF16)
    logits = lax.dot_general(
        bits[...], mixed[...], (((1,), (1,)), ((), ())), preferred_element_type=F32
    )
    chance = jax.nn.sigmoid(4.0 * (logits + offset[...]))
    probs[...] = chance
    row = lax.dot_general(
        jnp.ones((8, chance.shape[1]), F32),
        chance,
        (((1,), (1,)), ((), ())),
        preferred_element_type=F32,
        precision=lax.Precision.HIGHEST,
    )
    sums[...] = row[0:1]


def finish(pieces, shards, rows, bits, offset):
    count = rows.shape[0]
    return pl.pallas_call(
        finish_kernel,
        in_specs=[vmem()] + [pl.BlockSpec(memory_space=pl.ANY)] * 4 + [vmem()] * 7,
        out_specs=[vmem()] * 3,
        out_shape=[
            jax.ShapeDtypeStruct(rows.shape, BF16),
            jax.ShapeDtypeStruct((bits.shape[0], count), F32),
            jax.ShapeDtypeStruct((1, bits.shape[0]), F32),
        ],
        scratch_shapes=[
            pltpu.VMEM((2, 8, 4, 32, 512), BF16),
            pltpu.VMEM((count, 1024), BF16),
            pltpu.SemaphoreType.DMA((4,)),
        ],
        compiler_params=params(),
        name="finish",
    )(pieces, *shards, rows, bits, offset)


def on_device(
    residual_tiles,
    picture_label_tile,
    prenorm_multiplier,
    triple_projector,
    logit_scaling,
    final_projector,
    binarizer_projector,
    binarizer_offset,
):
    rows = residual_tiles[0]
    count, width = rows.shape
    core = lax.axis_index("seq_1")
    member = lax.axis_index(SEQ)
    def from_step(x, k, axis="seq_0"):
        length = lax.axis_size(axis)
        return lax.ppermute(x, axis, [(i, (i - k) % length) for i in range(length)])

    def from_other_core(x):
        return lax.ppermute(x, "seq_1", [(0, 1), (1, 0)])

    marked = jnp.pad(picture_label_tile.astype(BF16), ((0, 15), (0, width - count)))
    load = jnp.concatenate([rows, marked], axis=0)
    near = [load] + [from_step(load, k) for k in (1, 3, 2)]

    in_hbm = lambda x: pltpu.with_memory_space_constraint(x, pltpu.HBM)
    owned = pack(in_hbm(triple_projector), in_hbm(final_projector), lax.axis_size("dp_0"))
    owned = lax.all_to_all(owned, "dp_0", 0, 0, tiled=True)
    shard, mixing = spread(in_vmem(owned), lax.axis_size("dp_1"))
    shard, mixing = in_hbm(shard), in_hbm(mixing)
    shard = lax.all_to_all(shard, "dp_1", 0, 0, tiled=True)
    pieces = [x for own in near for x in (own, from_other_core(own))]
    mixing, _ = lax.optimization_barrier((mixing, shard))
    mixings = [mixing] + [from_step(mixing, k, "dp_1") for k in (2, 1, 3)]

    pieces, shard = in_vmem((pieces, shard))
    attended = layer(logit_scaling, prenorm_multiplier[None], pieces, shard)
    mixings, attended = lax.optimization_barrier((mixings, attended))
    mixings = [in_hbm(m) for m in mixings]
    mixings = mixings + in_vmem([from_other_core(m) for m in mixings])
    attended = lax.all_to_all(attended, SEQ, 0, 0, tiled=True)
    mixed, probs, sums = finish(
        in_vmem(attended),
        mixings,
        rows,
        binarizer_projector.T,
        binarizer_offset[:, None],
    )
    sums = jnp.sum(copy_for_each(sums, ("dp_0", "dp_1", "seq_0")), axis=(0, 1))
    marginal = (sums + from_other_core(sums)) / (count * lax.axis_size(ALL))
    code_entropy = -(marginal * jnp.log(marginal) + (1.0 - marginal) * jnp.log(1.0 - marginal))
    bit_codes = (probs - marginal[:, None])[None]
    return (mixed[None], bit_codes, code_entropy)


def solution(mesh):
    finer = Mesh(mesh.devices.reshape(8, 4, 4, 2), ("dp_0", "dp_1", "seq_0", "seq_1"))
    placed = (P(DP, SEQ, None), P(DP, SEQ), P(), P(DP, None), P(), P(DP, None), P(), P())
    return jax.shard_map(
        on_device,
        mesh=finer,
        in_specs=placed,
        out_specs=(P(DP, SEQ, None), P(DP, None, SEQ), P()),
        check_vma=False,
    )
```

```python
import functools
import math

import jax
import jax.numpy as jnp
from jax import lax
from jax.experimental import pallas as pl
from jax.experimental.pallas import tpu as pltpu
from jax.sharding import Mesh
from jax.sharding import PartitionSpec as P

SEQ = ("seq_0", "seq_1")
DP = ("dp_0", "dp_1")
ALL = ("dp_0", "dp_1", "seq_0", "seq_1")

EPS = 1e-06
EXCLUDED = -32768.0
KEYS = 512
ROWS = 256
SAFE = 8.0
LIMIT = 28 * 1024 * 1024
F32 = jnp.float32
BF16 = jnp.bfloat16


def params():
    return pltpu.CompilerParams(vmem_limit_bytes=LIMIT)


def vmem():
    return pl.BlockSpec(memory_space=pltpu.VMEM)


def smem():
    return pl.BlockSpec(memory_space=pltpu.SMEM)


def in_vmem(tree):
    return jax.tree.map(lambda x: pltpu.with_memory_space_constraint(x, pltpu.VMEM), tree)


def copy_for_each(x, axis):
    length = lax.axis_size(axis)
    return lax.all_to_all(jnp.broadcast_to(x[None], (length, *x.shape)), axis, 0, 0, tiled=True)


def pack_kernel(triple, final, out, held, sems):
    chip, core = lax.axis_index("seq_0"), lax.axis_index("seq_1")
    member = 2 * chip + core
    copies = [
        pltpu.make_async_copy(
            triple.at[:, pl.ds(pl.multiple_of(1024 * i + member * 128, 128), 128)],
            held.at[:, pl.ds(128 * i, 128)],
            sems.at[i],
        )
        for i in range(3)
    ]
    copies.append(
        pltpu.make_async_copy(
            final.at[:, pl.ds(pl.multiple_of(core * 512, 512), 512)],
            held.at[:, pl.ds(384, 512)],
            sems.at[3],
        )
    )
    for copy in copies:
        copy.start()
    for copy in copies:
        copy.wait()
    for i in range(out.shape[0]):
        out[i] = held[...]


def pack(triple, final, length):
    shard = triple.shape[0]
    anywhere = pl.BlockSpec(memory_space=pltpu.HBM)
    return pl.pallas_call(
        pack_kernel,
        in_specs=[anywhere, anywhere],
        out_specs=vmem(),
        out_shape=jax.ShapeDtypeStruct((length, shard, 896), BF16),
        scratch_shapes=[pltpu.VMEM((shard, 896), BF16), pltpu.SemaphoreType.DMA((4,))],
        compiler_params=params(),
        name="pack",
    )(triple, final)


def spread_kernel(both, shard, mixing):
    for i in range(shard.shape[0]):
        shard[i] = both[:, :, 0:384]
    mixing[...] = both[:, :, 384:896]


def spread(both, length):
    lead = both.shape[:2]
    return pl.pallas_call(
        spread_kernel,
        in_specs=[vmem()],
        out_specs=[vmem()] * 2,
        out_shape=[
            jax.ShapeDtypeStruct((length, *lead, 384), BF16),
            jax.ShapeDtypeStruct((*lead, 512), BF16),
        ],
        compiler_params=params(),
        name="spread",
    )(both)


def layer_kernel(scales, gain, *refs):
    pieces, shards, out = refs[:8], refs[8], refs[9]
    weights, normed, labels, queries, keys, values, total, even, odd, table = refs[10:]
    core, chip = lax.axis_index("seq_1"), lax.axis_index("seq_0")
    first = (2 * chip + core) * 2
    scale = [scales[first] / math.sqrt(64), scales[first + 1] / math.sqrt(64)]
    rows = ROWS
    for i in range(4):
        weights[:, i] = shards[i]
    head = 64
    matrix = weights[...].reshape(normed.shape[1], 384)
    lane = lax.broadcasted_iota(jnp.int32, (rows, 128), 1)
    spot = lax.broadcasted_iota(jnp.int32, (head, rows), 0)
    for pair in range(4):
        step = (0, 2, 1, 3)[pair]
        for side in range(2):
            wide = pieces[2 * pair + side][0:rows].astype(F32)
            inv = lax.rsqrt(jnp.mean(wide * wide, axis=-1, keepdims=True) + EPS)
            normed[side * rows : (side + 1) * rows] = (wide * inv * gain[...]).astype(BF16)
        both = jnp.dot(normed[...], matrix, preferred_element_type=F32).astype(BF16).astype(F32)
        for side in range(2):
            part = core if side == 0 else 1 - core
            block = 2 * lax.rem(chip + step, 4) + part
            start = pl.multiple_of(block * rows, rows)
            joined = both[side * rows : (side + 1) * rows]
            ids = pieces[2 * pair + side][rows : rows + 8, 0:rows].astype(F32)[0:1].astype(jnp.int32)
            labels[pl.ds(block, 1), :] = ids
            same = spot == ids
            bars = jnp.where(same, 0.0, EXCLUDED).astype(F32)
            query = joined[:, 0:128].T
            key = joined[:, 128:256].T
            marks = jnp.where(same, 1.0, 0.0).astype(BF16)
            for h in range(2):
                one = query[h * head : (h + 1) * head]
                inv = lax.rsqrt(jnp.mean(one * one, axis=0, keepdims=True) + EPS)
                queries[h, pl.ds(start, rows), :] = (
                    jnp.concatenate([one * inv * scale[h], bars], axis=0).T.astype(BF16)
                )
                one = key[h * head : (h + 1) * head]
                inv = lax.rsqrt(jnp.mean(one * one, axis=0, keepdims=True) + EPS)
                keys[h, 0:head, pl.ds(start, rows)] = (one * inv).astype(BF16)
                keys[h, head : 2 * head, pl.ds(start, rows)] = marks
            value = joined[:, 256:384]
            values[0, pl.ds(start, rows), :] = jnp.where(lane < head, value, 1.0).astype(BF16)
            values[1, pl.ds(start, rows), :] = jnp.where(
                lane < head, pltpu.roll(value, head, 1), 1.0
            ).astype(BF16)

    every = labels[...]
    opening, closing = every[:, 0:1], every[:, rows - 1 : rows]
    below = jnp.zeros((8, rows), jnp.int32)
    upto = jnp.zeros((8, rows), jnp.int32)
    for b in range(8):
        below += (every[b : b + 1] < opening).astype(jnp.int32)
        upto += (every[b : b + 1] <= closing).astype(jnp.int32)
    low = jnp.sum(below, axis=1, keepdims=True)
    high = jnp.sum(upto, axis=1, keepdims=True)
    low = low & -128
    counts = lax.shift_right_logical(high - low + (KEYS - 1), 9)
    low = jnp.minimum(low, 2048 - counts * KEYS)
    lows = [low[b, 0] for b in range(8)]
    counts = [counts[b, 0] for b in range(8)]
    total[...] = jnp.zeros(total.shape, F32)

    pairs = jnp.int32(0)
    for b in range(8):

        def note(s, pairs, b=b):
            table[0, pairs] = jnp.int32(b * rows)
            table[1, pairs] = lows[b] + s * KEYS
            return pairs + 1

        pairs = lax.fori_loop(0, counts[b], note, pairs)
    for spare in range(2):
        table[0, pairs + spare] = jnp.int32(8 * rows)
        table[1, pairs + spare] = jnp.int32(0)

    def score(j, into):
        row = pl.multiple_of(table[0, j], rows)
        key = pl.multiple_of(table[1, j], 128)
        for h in range(2):
            into[h] = jnp.dot(
                queries[h, pl.ds(row, rows), :],
                keys[h, :, pl.ds(key, KEYS)],
                preferred_element_type=F32,
            )

    def absorb(j, source):
        row = pl.multiple_of(table[0, j], rows)
        key = pl.multiple_of(table[1, j], 128)
        for h in range(2):
            total[h, pl.ds(row, rows), :] += jnp.dot(
                jnp.exp(source[h]).astype(BF16),
                values[h, pl.ds(key, KEYS), :],
                preferred_element_type=F32,
            )

    small = jnp.maximum(scales[first], scales[first + 1]) <= SAFE

    @pl.when(small)
    def _():
        score(0, even)

        def twice(j, carry):
            score(2 * j + 1, odd)
            absorb(2 * j, even)
            score(2 * j + 2, even)
            absorb(2 * j + 1, odd)
            return carry

        lax.fori_loop(0, (pairs + 1) // 2, twice, 0)

    @pl.when(jnp.logical_not(small))
    def _():
        for b in range(8):
            own = pl.ds(b * rows, rows)
            for h in range(2):

                def scores(j, b=b, h=h, own=own):
                    key = pl.multiple_of(lows[b] + j * KEYS, 128)
                    return key, jnp.dot(
                        queries[h, own, :], keys[h, :, pl.ds(key, KEYS)], preferred_element_type=F32
                    )

                def top(j, most, scores=scores):
                    return jnp.maximum(most, jnp.max(scores(j)[1], axis=-1, keepdims=True))

                largest = lax.fori_loop(
                    0, counts[b], top, jnp.full((rows, 1), 2.0 * EXCLUDED, F32)
                )

                def gather(j, carry, h=h, own=own, scores=scores, largest=largest):
                    key, found = scores(j)
                    total[h, own, :] += jnp.dot(
                        jnp.exp(found - largest).astype(BF16),
                        values[h, pl.ds(key, KEYS), :],
                        preferred_element_type=F32,
                    )
                    return carry

                lax.fori_loop(0, counts[b], gather, 0)

    for b in range(8):
        own = slice(b * rows, (b + 1) * rows)
        left, right = total[0, own, :], total[1, own, :]
        over = jnp.where(lane < head, left, pltpu.roll(right, head, 1))
        under = jnp.where(lane < head, pltpu.roll(left, head, 1), right)
        out[b] = (over / under).astype(BF16)


def layer(scales, gain, pieces, shard):
    total = 8 * ROWS
    return pl.pallas_call(
        layer_kernel,
        in_specs=[smem()] + [vmem()] * 10,
        out_specs=vmem(),
        out_shape=jax.ShapeDtypeStruct((8, ROWS, 128), BF16),
        scratch_shapes=[
            pltpu.VMEM((8, 4, 32, 384), BF16),
            pltpu.VMEM((2 * ROWS, pieces[0].shape[1]), BF16),
            pltpu.VMEM((8, ROWS), jnp.int32),
            pltpu.VMEM((2, total + ROWS, 128), BF16),
            pltpu.VMEM((2, 128, total), BF16),
            pltpu.VMEM((2, total, 128), BF16),
            pltpu.VMEM((2, total + ROWS, 128), F32),
            pltpu.VMEM((2, ROWS, KEYS), F32),
            pltpu.VMEM((2, ROWS, KEYS), F32),
            pltpu.SMEM((2, 48), jnp.int32),
        ],
        compiler_params=params(),
        name="layer",
    )(scales, gain, *pieces, shard)


def finish_kernel(pieces, *refs):
    shards, (rows, bits, offset, mixed, probs, sums, weights, joined, sems) = refs[:8], refs[8:]
    core, across = lax.axis_index("seq_1"), lax.axis_index("dp_1")
    copies = []
    for i in range(4):
        place = lax.rem(across + (0, 2, 1, 3)[i], 4)
        copies.append(
            pltpu.make_async_copy(shards[i], weights.at[core, :, place], sems.at[i])
        )
        copies[i].start()
    for i in range(4):
        place = lax.rem(across + (0, 2, 1, 3)[i], 4)
        weights[1 - core, :, place] = shards[4 + i][...]
    for source in range(8):
        joined[:, source * 128 : (source + 1) * 128] = pieces[source]
    for turn, part in ((0, 1 - core), (1, core)):
        if turn:
            for copy in copies:
                copy.wait()
        columns = pl.ds(pl.multiple_of(part * 512, 512), 512)
        moved = jnp.dot(
            joined[...], weights[part].reshape(1024, 512), preferred_element_type=F32
        )
        mixed[:, columns] = (rows[:, columns].astype(F32) + moved).astype(BF16)
    logits = lax.dot_general(
        bits[...], mixed[...], (((1,), (1,)), ((), ())), preferred_element_type=F32
    )
    chance = jax.nn.sigmoid(4.0 * (logits + offset[...]))
    probs[...] = chance
    row = lax.dot_general(
        jnp.ones((8, chance.shape[1]), F32),
        chance,
        (((1,), (1,)), ((), ())),
        preferred_element_type=F32,
        precision=lax.Precision.HIGHEST,
    )
    sums[...] = row[0:1]


def finish(pieces, shards, rows, bits, offset):
    count = rows.shape[0]
    return pl.pallas_call(
        finish_kernel,
        in_specs=[vmem()] + [pl.BlockSpec(memory_space=pl.ANY)] * 4 + [vmem()] * 7,
        out_specs=[vmem()] * 3,
        out_shape=[
            jax.ShapeDtypeStruct(rows.shape, BF16),
            jax.ShapeDtypeStruct((bits.shape[0], count), F32),
            jax.ShapeDtypeStruct((1, bits.shape[0]), F32),
        ],
        scratch_shapes=[
            pltpu.VMEM((2, 8, 4, 32, 512), BF16),
            pltpu.VMEM((count, 1024), BF16),
            pltpu.SemaphoreType.DMA((4,)),
        ],
        compiler_params=params(),
        name="finish",
    )(pieces, *shards, rows, bits, offset)


def on_device(
    residual_tiles,
    picture_label_tile,
    prenorm_multiplier,
    triple_projector,
    logit_scaling,
    final_projector,
    binarizer_projector,
    binarizer_offset,
):
    rows = residual_tiles[0]
    count, width = rows.shape
    core = lax.axis_index("seq_1")
    member = lax.axis_index(SEQ)
    def from_step(x, k, axis="seq_0"):
        length = lax.axis_size(axis)
        return lax.ppermute(x, axis, [(i, (i - k) % length) for i in range(length)])

    def from_other_core(x):
        return lax.ppermute(x, "seq_1", [(0, 1), (1, 0)])

    marked = jnp.pad(picture_label_tile.astype(BF16), ((0, 15), (0, width - count)))
    load = jnp.concatenate([rows, marked], axis=0)
    near = [load] + [from_step(load, k) for k in (2, 1, 3)]

    in_hbm = lambda x: pltpu.with_memory_space_constraint(x, pltpu.HBM)
    owned = pack(in_hbm(triple_projector), in_hbm(final_projector), lax.axis_size("dp_0"))
    owned = lax.all_to_all(owned, "dp_0", 0, 0, tiled=True)
    shard, mixing = spread(in_vmem(owned), lax.axis_size("dp_1"))
    shard, mixing = in_hbm(shard), in_hbm(mixing)
    shard = lax.all_to_all(shard, "dp_1", 0, 0, tiled=True)
    pieces = [x for own in near for x in (own, from_other_core(own))]
    mixing, _ = lax.optimization_barrier((mixing, shard))
    mixings = [mixing] + [from_step(mixing, k, "dp_1") for k in (2, 1, 3)]

    pieces, shard = in_vmem((pieces, shard))
    attended = layer(logit_scaling, prenorm_multiplier[None], pieces, shard)
    mixings, attended = lax.optimization_barrier((mixings, attended))
    mixings = [in_hbm(m) for m in mixings]
    mixings = mixings + in_vmem([from_other_core(m) for m in mixings])
    attended = lax.all_to_all(attended, SEQ, 0, 0, tiled=True)
    mixed, probs, sums = finish(
        in_vmem(attended),
        mixings,
        rows,
        binarizer_projector.T,
        binarizer_offset[:, None],
    )
    sums = jnp.sum(copy_for_each(sums, ("dp_0", "dp_1", "seq_0")), axis=(0, 1))
    marginal = (sums + from_other_core(sums)) / (count * lax.axis_size(ALL))
    code_entropy = -(marginal * jnp.log(marginal) + (1.0 - marginal) * jnp.log(1.0 - marginal))
    bit_codes = (probs - marginal[:, None])[None]
    return (mixed[None], bit_codes, code_entropy)


def solution(mesh):
    finer = Mesh(mesh.devices.reshape(8, 4, 4, 2), ("dp_0", "dp_1", "seq_0", "seq_1"))
    placed = (P(DP, SEQ, None), P(DP, SEQ), P(), P(DP, None), P(), P(DP, None), P(), P())
    return jax.shard_map(
        on_device,
        mesh=finer,
        in_specs=placed,
        out_specs=(P(DP, SEQ, None), P(DP, None, SEQ), P()),
        check_vma=False,
    )
```
